512 devices in a mesh: branch: 8 (over z), head: 32 (over x_lo, y, core), seq: 2 (over x_hi).
Axes of the slice: x: 4 (x_hi: 2, x_lo: 2; x = x_hi * 2 + x_lo), y: 8, z: 8, core: 2. Of those that a mesh axis runs over, the one named last changes fastest.
Arguments:
- text_hidden: bfloat16 [256, 4096], P('branch', 'head'), may hold values from -6 to 6
- text_length: int32 [1], replicated, may hold values from 64 to 256
- latent: bfloat16 [8, 1024, 6144], P('branch', 'seq', 'head'), may hold values from -26 to 26
- noise: bfloat16 [8, 1024, 6144], P('branch', 'seq', 'head'), may hold values from -6 to 6
- level_index: int32 [8], P('branch'), may hold values from 0 to 7
- mod_table: bfloat16 [4, 8, 3, 6144], replicated, may hold values from -10 to 10
- wq_halves: bfloat16 [8, 3072, 4096], P('branch', None, 'head'), may hold values from -0.078125 to 0.078125
- wo_halves: bfloat16 [8, 2048, 6144], P('branch', None, 'head'), may hold values from -19 to 19
- wkv_halves: bfloat16 [8, 2048, 2, 4096], P('branch', None, None, 'head'), may hold values from -2 to 2
Outputs:
- denoised: bfloat16 [8, 1024, 6144], P('branch', 'seq', 'head')
- clip_loss: float32 [8], P('branch')
The draws below stay inside these ranges and needn't reach their ends.
All inputs are finite; a program needn't handle non-finite values.
Results may differ from the reference program's by a relative error of at most 0.013.
Values may be sent and summed in bfloat16 or wider, within the bound.
A program may use at most 64 MiB of HBM per device.

```python
import math
import jax
import jax.numpy as jnp
from jax import lax

D = 6144
TD = 4096
HD = 128
HEADS = 32
TEXT_LEN = 256
LEVELS = 8
ATT = 4096
LEN = 1024
CLIPS = 8
BRANCHES = 4


def draw_latent(key, part):
    first_key, second_key = jax.random.split(key, 2)
    column_ramp = jnp.exp(math.log(3.0) * jnp.arange(D).astype(jnp.float32) / D)
    column_jitter = jnp.exp(jax.random.uniform(second_key, (D,), jnp.float32, -0.35, 0.35))
    column_scale = column_ramp * column_jitter
    base = jax.random.truncated_normal(first_key, -6.0, 6.0, (CLIPS, LEN, D), jnp.float32)
    values_out = base * column_scale
    return values_out.astype(jnp.bfloat16)


def head_factors(key):
    exponent = jax.random.uniform(jax.random.fold_in(key, 7001), (BRANCHES, HEADS), jnp.float32, -1.2, 1.2)
    return jnp.exp(exponent) / math.sqrt(math.sinh(2.4) / 2.4)


def draw_mod_table(key, part):
    base_key = jax.random.fold_in(key, 7005)
    shape_full = (BRANCHES, LEVELS, 3, D)
    base = jax.random.truncated_normal(base_key, -4.0, 4.0, shape_full, jnp.float32)
    channel_scale = jnp.array([1.0, 1.0, 2.5], jnp.float32)
    return (base * channel_scale[None, None, :, None]).astype(jnp.bfloat16)


def draw_wo_halves(key, part):
    factors = head_factors(key)
    clip_ids = jnp.arange(CLIPS)
    clip_branch = clip_ids // 2
    row_global = (clip_ids % 2)[:, None] * (ATT // 2) + jnp.arange(ATT // 2)[None, :]
    row_head = row_global // HD
    row_scale = factors[clip_branch[:, None], row_head]
    block_exponent = jax.random.uniform(jax.random.fold_in(key, 7002), (BRANCHES, HEADS, 32), jnp.float32, -2.0, 2.0)
    block_scale = jnp.exp(block_exponent) / math.sqrt(math.sinh(4.0) / 4.0)
    column_block = jnp.arange(D) * 32 // D
    per_row = block_scale[clip_branch[:, None], row_head]
    column_scale = per_row[:, :, column_block]
    base_key = jax.random.fold_in(key, 7003)
    shape_full = (CLIPS, ATT // 2, D)
    base = jax.random.truncated_normal(base_key, -6.0, 6.0, shape_full, jnp.float32)
    values_out = base * (row_scale * HD ** (-0.5))[:, :, None] * column_scale
    return values_out.astype(jnp.bfloat16)


def draw_wkv_halves(key, part):
    factors = head_factors(key)
    clip_branch = jnp.arange(CLIPS) // 2
    column_head = jnp.arange(ATT) // HD
    value_scale = factors[clip_branch[:, None], column_head[None, :]]
    slot_scale = jnp.stack([jnp.ones_like(value_scale), value_scale], axis=1)
    base_key = jax.random.fold_in(key, 7004)
    shape_full = (CLIPS, TD // 2, 2, ATT)
    base = jax.random.truncated_normal(base_key, -6.0, 6.0, shape_full, jnp.float32)
    values_out = base * TD ** (-0.5) * slot_scale[:, None, :, :]
    return values_out.astype(jnp.bfloat16)


def with_ends(drawn, key, smallest, top_value):
    longest = drawn.shape.index(max(drawn.shape))
    spots = []
    for shift in (0, 1):
        where = [jax.random.randint(jax.random.fold_in(key, axis), (), 0, length) for axis, length in enumerate(drawn.shape)]
        where[longest] = (where[longest] + shift) % drawn.shape[longest]
        spots.append(tuple(where))
    return drawn.at[spots[0]].set(smallest).at[spots[1]].set(top_value)


def steps_of(stream_key, shape, cuts, low, top_value):
    def one(axis_at, shards_of):
        draws = jax.random.uniform(jax.random.fold_in(jax.random.fold_in(stream_key, 6), axis_at), (shards_of,), jnp.float32, low / len(cuts), top_value / len(cuts))
        return jnp.repeat(jnp.exp(draws), shape[axis_at] // shards_of).reshape((-1,) + (1,) * (len(shape) - axis_at - 1))

    level = one(*cuts[0])
    for cut in cuts[1:]:
        level = level * one(*cut)
    return level


def normal_values(key, extent, width, bound, cuts=(), kind=jnp.bfloat16):
    entries = width * jax.random.normal(key, extent, jnp.float32)
    if cuts:
        entries = entries * steps_of(key, extent, cuts, -0.22, 0.18)
    return jnp.clip(entries, -bound, bound).astype(kind)


def setup_inputs(seed: int = 0) -> dict:
    splits = jax.random.split(jax.random.key(seed), 10)
    return {
        "text_hidden": normal_values(splits[0], (TEXT_LEN, TD), 1.0, 6.0, ((0, 8), (1, 32))),
        "text_length": jax.random.randint(splits[1], (1,), TEXT_LEN // 4, TEXT_LEN + 1).astype(jnp.int32),
        "latent": draw_latent(jax.random.fold_in(splits[9], 71), 0),
        "noise": normal_values(splits[3], (CLIPS, LEN, D), 1.0, 6.0, ((0, 8), (1, 2), (2, 32))),
        "level_index": with_ends(jax.random.randint(splits[4], (CLIPS,), 0, LEVELS), jax.random.fold_in(splits[4], 1), 0, LEVELS - 1).astype(jnp.int32),
        "mod_table": draw_mod_table(jax.random.fold_in(splits[9], 71), 0),
        "wq_halves": normal_values(splits[6], (CLIPS, D // 2, ATT), D ** -0.5, 0.078125, ((0, 8), (2, 32))),
        "wo_halves": draw_wo_halves(jax.random.fold_in(splits[9], 71), 0),
        "wkv_halves": draw_wkv_halves(jax.random.fold_in(splits[9], 71), 0),
    }


epsilon = 1e-06
sigma_min = 1e-05

def head_norm(values_in):
    return values_in * lax.rsqrt(lax.optimization_barrier(jnp.mean(values_in * values_in, axis=-1, keepdims=True)) + epsilon)

def reference(text_hidden, text_length, latent, noise, level_index, mod_table, wq_halves, wo_halves, wkv_halves):
    text_float = text_hidden.astype(jnp.float32)
    mean_square = lax.optimization_barrier(jnp.mean(text_float * text_float, axis=1, keepdims=True))
    text_normed = (text_float * lax.rsqrt(mean_square + epsilon)).astype(jnp.bfloat16)
    w_query = wq_halves.reshape(BRANCHES, D, ATT)
    w_output = wo_halves.reshape(BRANCHES, ATT, D)
    w_text = wkv_halves.reshape(BRANCHES, TD, 2 * ATT)
    live_keys = (jnp.arange(TEXT_LEN) < text_length[0]).astype(jnp.float32)
    level_times = (jnp.arange(LEVELS).astype(jnp.float32) + 0.5) / LEVELS
    layer_outs = []
    losses = []
    for clip_at in range(CLIPS):
        branch = clip_at // 2
        text_proj = jnp.dot(text_normed, w_text[branch], preferred_element_type=jnp.float32)
        text_proj = text_proj.reshape(TEXT_LEN, 2, HEADS, HD)
        text_keys = head_norm(text_proj[:, 0]).astype(jnp.bfloat16)
        text_values = text_proj[:, 1].astype(jnp.bfloat16)
        onehot = (jnp.arange(LEVELS) == level_index[clip_at]).astype(jnp.float32)
        level_time = jnp.sum(onehot * level_times)
        modulation = jnp.einsum('l,lcd->cd', onehot, mod_table[branch].astype(jnp.float32))
        clean_float = latent[clip_at].astype(jnp.float32)
        noise_float = noise[clip_at].astype(jnp.float32)
        noisy = (level_time * clean_float + (1.0 - (1.0 - sigma_min) * level_time) * noise_float).astype(jnp.bfloat16)
        noisy_float = noisy.astype(jnp.float32)
        row_mean = lax.optimization_barrier(jnp.mean(noisy_float, axis=1, keepdims=True))
        row_var = lax.optimization_barrier(jnp.mean(noisy_float * noisy_float, axis=1, keepdims=True)) - row_mean * row_mean
        modulated = ((noisy_float - row_mean) * lax.rsqrt(row_var + epsilon) * (1.0 + modulation[1]) + modulation[0]).astype(jnp.bfloat16)
        queries = jnp.dot(modulated, w_query[branch], preferred_element_type=jnp.float32).reshape(LEN, HEADS, HD)
        queries = head_norm(queries).astype(jnp.bfloat16)
        scores = jnp.einsum('rhd,thd->hrt', queries.astype(jnp.float32), text_keys.astype(jnp.float32)) / jnp.sqrt(jnp.float32(HD))
        weights_exp = jnp.exp(scores) * live_keys
        attn_weights = (weights_exp / lax.optimization_barrier(jnp.sum(weights_exp, axis=-1, keepdims=True))).astype(jnp.bfloat16)
        attended = jnp.einsum('hrt,thd->rhd', attn_weights.astype(jnp.float32), text_values.astype(jnp.float32))
        attended = attended.astype(jnp.bfloat16).reshape(LEN, ATT)
        projected = jnp.dot(attended, w_output[branch], preferred_element_type=jnp.float32)
        denoised = (noisy_float + modulation[2] * projected).astype(jnp.bfloat16)
        target = clean_float - (1.0 - sigma_min) * noise_float
        errors = denoised.astype(jnp.float32) - target
        layer_outs.append(denoised)
        losses.append(jnp.mean(errors * errors))
    return (jnp.stack(layer_outs), jnp.stack(losses))
```

```python
import jax
import jax.numpy as jnp
from jax import lax
from jax.experimental import pallas as pl
from jax.experimental.pallas import tpu as pltpu
from jax.sharding import PartitionSpec as P

MESH = pl.DeviceIdType.MESH
F32 = jnp.float32
BF16 = jnp.bfloat16

D = 6144
TD = 4096
HD = 128
LEVELS = 8
YN = 8
ZN = 8
CH = 192
TOK = 256
epsilon = 1e-06
sigma_min = 1e-05

ORDER = (0, 1, 7, 2, 6, 3, 5, 4)


def hid(x, y, c):
    return x * 16 + y * 2 + c


def kernel(
    level_ref,
    length_ref,
    text_ref,
    lat_ref,
    noi_ref,
    mod_hbm,
    wq_hbm,
    wo_hbm,
    wkv_hbm,
    out_ref,
    loss_ref,
    modv,
    wqv,
    wkv2,
    wkvf,
    wkv,
    wo,
    wq,
    nz,
    xsend,
    rows,
    gcol,
    tx,
    kvs,
    kvr,
    kvb,
    pacc,
    uacc,
    vacc,
    s1acc,
    s2acc,
    att,
    oacc,
    xs2,
    xr2,
    l1,
    l2,
    lsem,
    wosem,
    t1s,
    t1r,
    t2s,
    t2r,
    tss,
    tsr,
    xes,
    xer,
    r1s,
    r1r,
    b1s,
    b1r,
    wzs,
    wzr,
    wts,
    wtr,
    wfs,
    wfr,
    kzs,
    kzr,
    kxs,
    kxr,
    r2s,
    r2r,
    b2s,
    b2r,
    ozs,
    ozr,
    ots,
    otr,
    ofs,
    ofr,
    xfs,
    xfr,
    l1s,
    l1r,
    l2s,
    l2r,
):
    h = lax.axis_index("head")
    z = lax.axis_index("branch")
    s = lax.axis_index("seq")
    c = lax.rem(h, 2)
    y = lax.rem(lax.div(h, 2), YN)
    x = lax.div(h, 16)
    p = lax.rem(z, 2)
    nx = 1 - x
    np_ = 1 - p

    def yy(off):
        return lax.rem(y + off, YN)

    def rcopy(src, dst, ssem, rsem, dev):
        return pltpu.make_async_remote_copy(
            src_ref=src, dst_ref=dst, send_sem=ssem, recv_sem=rsem,
            device_id=dev, device_id_type=MESH,
        )

    sib = {"head": hid(x, y, 1 - c)}
    up = {"head": hid(x, yy(1), c)}
    down = {"head": hid(x, yy(7), c)}
    inner = {"head": hid(nx, y, c)}
    outer = {"head": hid(nx, y, c), "seq": 1 - s}
    far = {"seq": 1 - s}
    zpart = {"branch": z + 1 - 2 * p}

    cp_mod = pltpu.make_async_copy(mod_hbm.at[lax.div(z, 2)], modv, lsem.at[0])
    cp_wq = pltpu.make_async_copy(wq_hbm, wqv, lsem.at[1])
    cp_wkv = pltpu.make_async_copy(wkv_hbm, wkv2, lsem.at[2])
    cp_wq.start()
    cp_mod.start()
    cp_wkv.start()

    def cp_wo(i):
        return pltpu.make_async_copy(
            wo_hbm.at[:, pl.ds(i * 256, 256)], wo.at[x, p, i], wosem.at[i]
        )

    for i in range(YN):
        cp_wo(i).start()

    barrier = pltpu.get_barrier_semaphore()
    peers = []
    for dz in range(ZN):
        for x2 in range(2):
            zt = lax.rem(z + dz, ZN)
            if dz == 0:
                if x2 == 0:
                    peers.append(inner)
            else:
                peers.append({"branch": zt, "head": hid(x2, y, c)})
    for off in range(1, YN):
        peers.append({"head": hid(x, yy(off), c)})
    peers.append(sib)
    peers.append({"head": hid(nx, y, 1 - c)})
    for xx in (x, nx):
        for cc in (c, 1 - c):
            peers.append({"head": hid(xx, y, cc), "seq": 1 - s})
    for dev in peers:
        pl.semaphore_signal(barrier, inc=1, device_id=dev, device_id_type=MESH)

    level_time = (level_ref[0].astype(F32) + 0.5) / LEVELS
    noise_level = 1.0 - (1.0 - sigma_min) * level_time
    mine = pl.ds(pl.multiple_of(x * TOK, TOK), TOK)
    theirs = pl.ds(pl.multiple_of(nx * TOK, TOK), TOK)

    def noisy_of(cols):
        return (
            level_time * lat_ref[:, cols].astype(F32)
            + noise_level * noi_ref[:, cols].astype(F32)
        ).astype(BF16)

    nz[h] = noisy_of(mine)
    xsend[...] = noisy_of(theirs)
    text_rows = pl.ds(pl.multiple_of(s * 16, 16), 16)
    my_rows = pl.ds(pl.multiple_of(z * 16, 16), 16)
    my_lanes = pl.ds(pl.multiple_of(c * 128, 128), 128)

    @pl.when(x == p)
    def _():
        tx[y, my_rows, my_lanes] = text_ref[text_rows, :]

    cp_wq.wait()

    def turn(i, carry):
        block = wqv[pl.ds(pl.multiple_of(i * 384, 384), 384), :]
        wq[x, p, i] = jnp.transpose(block.astype(F32)).astype(BF16)
        return carry

    lax.fori_loop(0, YN, turn, 0)

    pl.semaphore_wait(barrier, len(peers))

    def t1(j, x2):
        return rcopy(
            text_ref.at[text_rows, :], tx.at[y, my_rows, my_lanes],
            t1s.at[j, x2], t1r.at[z],
            {"branch": 2 * j + x, "head": hid(x2, y, c)},
        )

    def t1_remote(j, x2):
        return jnp.logical_or(2 * j + x != z, x2 != x)

    for j in range(4):
        for x2 in range(2):
            @pl.when(t1_remote(j, x2))
            def _(j=j, x2=x2):
                t1(j, x2).start()

    xe = rcopy(xsend, nz.at[h], xes, xer, inner)
    xe.start()

    def piece(buf, x2, y2):
        return buf.at[hid(x2, y2, c)]

    def ring(buf, ssem, rsem, x2, y2, way):
        at = piece(buf, x2, y2)
        return rcopy(at, at, ssem.at[x2, y2, way], rsem.at[x2, y2], up if way == 0 else down)

    def bridge(buf, ssem, rsem, x2, y2):
        at = piece(buf, x2, y2)
        return rcopy(at, at, ssem.at[x2, y2], rsem.at[x2, y2], sib)

    def launch(buf, rs, rr, bs, br, x2):
        ring(buf, rs, rr, x2, y, 0).start()
        ring(buf, rs, rr, x2, y, 1).start()
        bridge(buf, bs, br, x2, y).start()

    launch(nz, r1s, r1r, b1s, b1r, x)

    def w_z(buf, ssem, rsem, i):
        at = buf.at[x, p, i]
        return rcopy(at, at, ssem.at[i], rsem.at[i], zpart)

    def w_out(buf, ssem, rsem, i):
        at = buf.at[x, p, i]
        return rcopy(at, at, ssem.at[i], rsem.at[i], outer)

    def w_fwd(buf, ssem, rsem, i):
        at = buf.at[x, np_, i]
        return rcopy(at, at, ssem.at[i], rsem.at[i], inner)

    for off in ORDER:
        w_z(wq, wzs, wzr, yy(off)).start()
        w_out(wq, wts, wtr, yy(off)).start()

    cp_mod.wait()
    pick = (lax.broadcasted_iota(jnp.int32, (LEVELS, 1), 0) == level_ref[0]).astype(F32)
    for k in range(3):
        for i in range(16):
            row = jnp.sum(
                modv[k, :, i * 384 : (i + 1) * 384].astype(F32) * pick, axis=0, keepdims=True
            )
            rows[k, i] = row + 1.0 if k == 1 else row
    for x2 in range(2):
        gate = jnp.broadcast_to(rows[2, x2 * 8 + y], (128, 384))
        gcol[x2] = jnp.transpose(gate)

    def t1_wait(zs):
        rcopy(
            text_ref.at[text_rows, :],
            tx.at[y, pl.ds(zs * 16, 16), my_lanes],
            t1s.at[0, 0], t1r.at[zs], inner,
        ).wait_recv()

    for zs in range(ZN):
        @pl.when(jnp.logical_or(x != p, z != zs))
        def _(zs=zs):
            t1_wait(zs)

    def t2(off):
        at = tx.at[y, :, my_lanes]
        return rcopy(at, at, t2s.at[off], t2r.at[y], {"head": hid(x, yy(off), c)})

    def t2_wait(y2):
        at = tx.at[y2, :, my_lanes]
        rcopy(at, at, t2s.at[0], t2r.at[y2], sib).wait_recv()

    def t_sib(y2):
        at = tx.at[y2, :, my_lanes]
        return rcopy(at, at, tss.at[y2], tsr.at[y2], sib)

    def t_sib_wait(y2):
        at = tx.at[y2, :, pl.ds(pl.multiple_of((1 - c) * 128, 128), 128)]
        rcopy(at, at, tss.at[y2], tsr.at[y2], sib).wait_recv()

    for off in (4, 3, 5, 2, 6, 1, 7):
        t2(off).start()
    t_sib(y).start()

    xe_in = rcopy(xsend, nz.at[hid(nx, y, c)], xes, xer, inner)
    xe_in.wait_recv()
    launch(nz, r1s, r1r, b1s, b1r, nx)

    cp_wkv.wait()

    def spread(i, carry):
        at = pl.ds(pl.multiple_of(i * 512, 512), 512)
        wkvf[...] = wkv2[at, :].astype(F32)
        to = pl.ds(pl.multiple_of(i * 256, 256), 256)
        wkv[to, 0:128] = wkvf[pl.ds(0, 256, stride=2), :].astype(BF16)
        wkv[to, 128:256] = wkvf[pl.ds(1, 256, stride=2), :].astype(BF16)
        return carry

    lax.fori_loop(0, YN, spread, 0)

    pacc[...] = jnp.zeros_like(pacc)
    uacc[...] = jnp.zeros_like(uacc)
    vacc[...] = jnp.zeros_like(vacc)
    s1acc[...] = jnp.zeros_like(s1acc)
    s2acc[...] = jnp.zeros_like(s2acc)

    def project(x2, y2):
        chip = x2 * 8 + y2
        n = nz[pl.ds(hid(x2, y2, 0), 2)].reshape(384, TOK)
        scale = rows[1, chip]
        shift = rows[0, chip]
        for g in range(2):
            w = wq[g, x2, y2].astype(F32)
            ws = w * scale
            high = ws.astype(BF16)
            low = (ws - high.astype(F32)).astype(BF16)
            pacc[g] += jnp.dot(high, n, preferred_element_type=F32) + jnp.dot(
                low, n, preferred_element_type=F32
            )
            uacc[g] += ws[:, 0:128] + ws[:, 128:256] + ws[:, 256:384]
            sh = w * shift
            vacc[g] += sh[:, 0:128] + sh[:, 128:256] + sh[:, 256:384]
        nf = n.astype(F32).reshape(48, 8, TOK)
        s1acc[...] += jnp.sum(nf, axis=0)
        s2acc[...] += jnp.sum(nf * nf, axis=0)

    def ring_step(buf, rs, rr, bs, br, k):
        for x2 in range(2):
            if k < 4 or x2 == 0:
                ring(buf, rs, rr, x2, yy(8 - k), 0).wait_recv()
                if k < 3 or (k == 3 and x2 == 0):
                    ring(buf, rs, rr, x2, yy(8 - k), 0).start()
                bridge(buf, bs, br, x2, yy(8 - k)).start()
            if k < 4 or x2 == 1:
                ring(buf, rs, rr, x2, yy(k), 1).wait_recv()
                if k < 3 or (k == 3 and x2 == 1):
                    ring(buf, rs, rr, x2, yy(k), 1).start()
                bridge(buf, bs, br, x2, yy(k)).start()

    def bridge_wait(buf, bs, br, y2):
        for x2 in range(2):
            at = buf.at[hid(x2, y2, 1 - c)]
            rcopy(at, at, bs.at[x2, y2], br.at[x2, y2], sib).wait_recv()

    def fwd_wait(buf, fs, fr, i):
        at = buf.at[nx, np_, i]
        rcopy(at, at, fs.at[i], fr.at[i], inner).wait_recv()

    def out_wait(buf, os_, or_, i):
        at = buf.at[nx, p, i]
        rcopy(at, at, os_.at[i], or_.at[i], outer).wait_recv()

    def z_forward(buf, zs, zr, fs, fr, i):
        at = buf.at[x, np_, i]
        rcopy(at, at, zs.at[i], zr.at[i], zpart).wait_recv()
        w_fwd(buf, fs, fr, i).start()

    def offsets(k):
        return (k,) if k in (0, 4) else (k, 8 - k)

    def query_block(k):
        for off in offsets(k):
            i = yy(off)
            bridge_wait(nz, b1s, b1r, i)
            out_wait(wq, wts, wtr, i)
            project(p, i)
            fwd_wait(wq, wfs, wfr, i)
            project(np_, i)

    def wq_forward(k):
        for off in offsets(k):
            z_forward(wq, wzs, wzr, wfs, wfr, yy(off))

    wq_forward(0)
    ring_step(nz, r1s, r1r, b1s, b1r, 1)
    for off in (1, 7, 2, 6, 3, 5, 4):
        t2_wait(yy(off))
        t_sib(yy(off)).start()
    wq_forward(1)
    query_block(0)
    ring_step(nz, r1s, r1r, b1s, b1r, 2)
    for y2 in range(YN):
        t_sib_wait(y2)

    kvs[0:128, :] = jnp.zeros((128, 256), F32)
    squares = jnp.zeros((128, 256), F32)
    for y2 in range(YN):
        t = tx[y2]
        kvs[0:128, :] += jnp.dot(
            t, wkv[y2 * 256 : (y2 + 1) * 256, :], preferred_element_type=F32
        )
        tf = t.astype(F32)
        squares = squares + tf * tf
    square_col = jnp.sum(squares, axis=1, keepdims=True)
    square_row = jnp.transpose(jnp.broadcast_to(square_col, (128, 128)))[0:8]
    kvs[128:136, 0:128] = square_row
    kvs[128:136, 128:256] = square_row
    kz = rcopy(kvs, kvr, kzs, kzr, zpart)
    kz.start()

    wq_forward(2)
    query_block(1)
    ring_step(nz, r1s, r1r, b1s, b1r, 3)
    wq_forward(3)

    kz.wait_recv()
    other_col = jnp.transpose(jnp.broadcast_to(kvr[128:129, 0:128], (128, 128)))[:, 0:1]
    text_rstd = lax.rsqrt((square_col + other_col) / TD + epsilon)
    text_proj = (kvs[0:128, :] + kvr[0:128, :]) * text_rstd
    keys = text_proj[:, 0:128]
    keys = keys * lax.rsqrt(jnp.mean(keys * keys, axis=1, keepdims=True) + epsilon)
    kvb[x, s, 0] = keys.astype(BF16)
    kvb[x, s, 1] = jnp.transpose(text_proj[:, 128:256]).astype(BF16)
    kx = [
        rcopy(kvb.at[x, s], kvb.at[x, s], kxs.at[k], kxr.at[x, s], dev)
        for k, dev in enumerate((inner, far, outer))
    ]
    for copy in kx:
        copy.start()

    for i in range(YN):
        cp_wo(i).wait()
    wq_forward(4)
    for off in ORDER:
        w_z(wo, ozs, ozr, yy(off)).start()
        w_out(wo, ots, otr, yy(off)).start()
    query_block(2)
    ring_step(nz, r1s, r1r, b1s, b1r, 4)
    query_block(3)
    query_block(4)

    for x2, s2 in ((nx, s), (x, 1 - s), (nx, 1 - s)):
        at = kvb.at[x2, s2]
        rcopy(at, at, kxs.at[0], kxr.at[x2, s2], inner).wait_recv()
    mean_row = jnp.sum(s1acc[...], axis=0, keepdims=True) / D
    var_row = jnp.sum(s2acc[...], axis=0, keepdims=True) / D - mean_row * mean_row
    rstd = lax.rsqrt(var_row + epsilon)
    index = lax.broadcasted_iota(jnp.int32, (128, TOK), 0)
    position = lax.div(index, 16) * 32 + lax.rem(index, 16)
    for g in range(2):
        u = jnp.sum(uacc[g], axis=1, keepdims=True)
        v = jnp.sum(vacc[g], axis=1, keepdims=True)
        q = (pacc[g] - u * mean_row) * rstd + v
        q = (q * lax.rsqrt(jnp.mean(q * q, axis=0, keepdims=True) + epsilon)).astype(BF16)
        exps = []
        for s2 in range(2):
            scores = jnp.dot(kvb[g, s2, 0], q, preferred_element_type=F32) / jnp.sqrt(F32(HD))
            live = position + 16 * s2 < length_ref[0]
            exps.append(jnp.where(live, jnp.exp(scores), 0.0))
        total = jnp.sum(exps[0], axis=0, keepdims=True) + jnp.sum(exps[1], axis=0, keepdims=True)
        inverse = 1.0 / total
        mixed = jnp.dot(
            kvb[g, 0, 1], (exps[0] * inverse).astype(BF16), preferred_element_type=F32
        ) + jnp.dot(kvb[g, 1, 1], (exps[1] * inverse).astype(BF16), preferred_element_type=F32)
        att[hid(g, y, c)] = mixed.astype(BF16)
        launch(att, r2s, r2r, b2s, b2r, g)

    oacc[...] = jnp.zeros_like(oacc)

    def out_project(x2, y2):
        a = att[pl.ds(hid(x2, y2, 0), 2)].reshape(256, TOK)
        for g in range(2):
            oacc[g] += jnp.dot(wo[g, x2, y2], a, preferred_element_type=F32)

    def out_block(k):
        for off in offsets(k):
            i = yy(off)
            bridge_wait(att, b2s, b2r, i)
            out_wait(wo, ots, otr, i)
            out_project(p, i)
            fwd_wait(wo, ofs, ofr, i)
            out_project(np_, i)

    def wo_forward(k):
        for off in offsets(k):
            z_forward(wo, ozs, ozr, ofs, ofr, yy(off))

    wo_forward(0)
    ring_step(att, r2s, r2r, b2s, b2r, 1)
    wo_forward(1)
    out_block(0)
    ring_step(att, r2s, r2r, b2s, b2r, 2)
    wo_forward(2)
    out_block(1)
    ring_step(att, r2s, r2r, b2s, b2r, 3)
    wo_forward(3)
    ring_step(att, r2s, r2r, b2s, b2r, 4)
    wo_forward(4)
    out_block(2)
    out_block(3)
    out_block(4)

    half = pl.ds(pl.multiple_of(c * CH, CH), CH)

    def denoise(x2):
        gate = gcol[x2, half, :]
        gated = oacc[x2] * jnp.concatenate([gate, gate], axis=1)
        return (nz[hid(x2, y, c)].astype(F32) + gated).astype(BF16)

    def error_of(done, cols):
        target = lat_ref[:, cols].astype(F32) - (1.0 - sigma_min) * noi_ref[:, cols].astype(F32)
        e = done.astype(F32) - target
        e = e * e
        e = jnp.sum(e.reshape(CH // 8, 8, TOK), axis=0)
        return e[:, 0:128] + e[:, 128:256]

    xs2[...] = denoise(nx)
    xf = rcopy(xs2, xr2, xfs, xfr, inner)
    xf.start()
    done = denoise(x)
    out_ref[:, mine] = done
    error = error_of(done, mine)
    xf.wait_recv()
    done = xr2[...]
    out_ref[:, theirs] = done
    error = error + error_of(done, theirs)

    def slot(ss, xx, cc):
        return ss * 4 + xx * 2 + cc

    here = slot(s, x, c)
    l1[here] = error
    group = []
    for ds in range(2):
        for dx in range(2):
            for dc in range(2):
                if ds + dx + dc:
                    s2 = s if ds == 0 else 1 - s
                    x2 = x if dx == 0 else nx
                    c2 = c if dc == 0 else 1 - c
                    group.append((s2, x2, c2))
    for k, (s2, x2, c2) in enumerate(group):
        rcopy(
            l1.at[here], l1.at[here], l1s.at[k], l1r.at[here], {"head": hid(x2, y, c2), "seq": s2}
        ).start()
    for s2, x2, c2 in group:
        at = l1.at[slot(s2, x2, c2)]
        rcopy(at, at, l1s.at[0], l1r.at[slot(s2, x2, c2)], sib).wait_recv()
    l2[y] = jnp.sum(l1[...], axis=0)
    for off in range(1, YN):
        rcopy(
            l2.at[y], l2.at[y], l2s.at[off], l2r.at[y], {"head": hid(x, yy(off), c)}
        ).start()

    for j in range(4):
        for x2 in range(2):
            @pl.when(t1_remote(j, x2))
            def _(j=j, x2=x2):
                t1(j, x2).wait_send()
    xe.wait_send()
    for off in range(1, YN):
        t2(off).wait_send()
    kz.wait_send()
    for copy in kx:
        copy.wait_send()
    xf.wait_send()

    for i in range(YN):
        t_sib(i).wait_send()
        w_z(wq, wzs, wzr, i).wait_send()
        w_out(wq, wts, wtr, i).wait_send()
        w_fwd(wq, wfs, wfr, i).wait_send()
        w_z(wo, ozs, ozr, i).wait_send()
        w_out(wo, ots, otr, i).wait_send()
        w_fwd(wo, ofs, ofr, i).wait_send()
        for x2 in range(2):
            bridge(nz, b1s, b1r, x2, i).wait_send()
            bridge(att, b2s, b2r, x2, i).wait_send()
    for buf, rs, rr in ((nz, r1s, r1r), (att, r2s, r2r)):
        for x2 in range(2):
            for k in range(4):
                if k < 3 or x2 == 0:
                    ring(buf, rs, rr, x2, yy(8 - k), 0).wait_send()
                if k < 3 or x2 == 1:
                    ring(buf, rs, rr, x2, yy(k), 1).wait_send()
    for k, (s2, x2, c2) in enumerate(group):
        rcopy(l1.at[here], l1.at[here], l1s.at[k], l1r.at[here], sib).wait_send()

    for off in range(1, YN):
        at = l2.at[yy(off)]
        rcopy(at, at, l2s.at[off], l2r.at[yy(off)], sib).wait_recv()
    for off in range(1, YN):
        rcopy(l2.at[y], l2.at[y], l2s.at[off], l2r.at[y], sib).wait_send()
    loss_ref[0] = jnp.sum(jnp.sum(l2[...], axis=0)) / (1024 * D)


def local(
    text_hidden, text_length, latent, noise, level_index, mod_table, wq_halves, wo_halves, wkv_halves
):
    dma = pltpu.SemaphoreType.DMA
    vmem = pltpu.VMEM
    any_ = pl.BlockSpec(memory_space=pl.ANY)
    in_vmem = pl.BlockSpec(memory_space=pltpu.VMEM)
    in_smem = pl.BlockSpec(memory_space=pltpu.SMEM)
    out, loss = pl.pallas_call(
        kernel,
        out_shape=(
            jax.ShapeDtypeStruct((CH, 2 * TOK), BF16),
            jax.ShapeDtypeStruct((1,), F32),
        ),
        in_specs=[in_smem, in_smem, in_vmem, in_vmem, in_vmem, any_, any_, any_, any_],
        out_specs=(in_vmem, in_smem),
        scratch_shapes=[
            vmem((3, LEVELS, D), BF16),
            vmem((D // 2, HD), BF16),
            vmem((TD, HD), BF16),
            vmem((512, HD), F32),
            vmem((TD // 2, 256), BF16),
            vmem((2, 2, YN, CH, 256), BF16),
            vmem((2, 2, YN, HD, 384), BF16),
            vmem((32, CH, TOK), BF16),
            vmem((CH, TOK), BF16),
            vmem((3, 16, 1, 384), F32),
            vmem((2, 384, 128), F32),
            vmem((YN, 128, 256), BF16),
            vmem((136, 256), F32),
            vmem((136, 256), F32),
            vmem((2, 2, 2, 128, 128), BF16),
            vmem((2, HD, TOK), F32),
            vmem((2, HD, 128), F32),
            vmem((2, HD, 128), F32),
            vmem((8, TOK), F32),
            vmem((8, TOK), F32),
            vmem((32, HD, TOK), BF16),
            vmem((2, CH, TOK), F32),
            vmem((CH, TOK), BF16),
            vmem((CH, TOK), BF16),
            vmem((8, 8, 128), F32),
            vmem((YN, 8, 128), F32),
            dma((3,)),
            dma((YN,)),
            dma((4, 2)),
            dma((ZN,)),
            dma((YN,)),
            dma((YN,)),
            dma((YN,)),
            dma((YN,)),
            dma,
            dma,
            dma((2, YN, 2)),
            dma((2, YN)),
            dma((2, YN)),
            dma((2, YN)),
            dma((YN,)),
            dma((YN,)),
            dma((YN,)),
            dma((YN,)),
            dma((YN,)),
            dma((YN,)),
            dma,
            dma,
            dma((3,)),
            dma((2, 2)),
            dma((2, YN, 2)),
            dma((2, YN)),
            dma((2, YN)),
            dma((2, YN)),
            dma((YN,)),
            dma((YN,)),
            dma((YN,)),
            dma((YN,)),
            dma((YN,)),
            dma((YN,)),
            dma,
            dma,
            dma((7,)),
            dma((8,)),
            dma((YN,)),
            dma((YN,)),
        ],
        compiler_params=pltpu.CompilerParams(
            collective_id=0, has_side_effects=True, vmem_limit_bytes=48 << 20
        ),
    )(
        level_index,
        text_length,
        text_hidden,
        jnp.swapaxes(latent[0], 0, 1),
        jnp.swapaxes(noise[0], 0, 1),
        jnp.swapaxes(mod_table, 1, 2),
        wq_halves[0],
        jnp.swapaxes(wo_halves[0], 0, 1),
        wkv_halves[0].reshape(TD, HD),
    )
    return (jnp.swapaxes(out, 0, 1)[None], loss)


def solution(mesh):
    return jax.shard_map(
        local,
        mesh=mesh,
        in_specs=(
            P("branch", "head"),
            P(),
            P("branch", "seq", "head"),
            P("branch", "seq", "head"),
            P("branch"),
            P(),
            P("branch", None, "head"),
            P("branch", None, "head"),
            P("branch", None, None, "head"),
        ),
        out_specs=(P("branch", "seq", "head"), P("branch")),
        check_vma=False,
    )
```

```python
import jax
import jax.numpy as jnp
from jax import lax
from jax.experimental import pallas as pl
from jax.experimental.pallas import tpu as pltpu
from jax.sharding import PartitionSpec as P

MESH = pl.DeviceIdType.MESH
F32 = jnp.float32
BF16 = jnp.bfloat16

D = 6144
TD = 4096
HD = 128
LEVELS = 8
YN = 8
ZN = 8
CH = 192
TOK = 256
epsilon = 1e-06
sigma_min = 1e-05

ORDER = (0, 1, 7, 2, 6, 3, 5, 4)


def hid(x, y, c):
    return x * 16 + y * 2 + c


def kernel(
    level_hbm,
    length_hbm,
    text_hbm,
    lat_hbm,
    noi_hbm,
    mod_hbm,
    wq_hbm,
    wo_hbm,
    wkv_hbm,
    out_ref,
    loss_ref,
    level_ref,
    length_ref,
    text_ref,
    lat_ref,
    noi_ref,
    modv,
    wqv,
    wkv2,
    wkvf,
    wkv,
    wo,
    wq,
    nz,
    nlat,
    nnoi,
    rows,
    gcol,
    tx,
    kvs,
    kvr,
    kvb,
    pacc,
    uacc,
    vacc,
    s1acc,
    s2acc,
    att,
    oacc,
    xs2,
    xr2,
    l1,
    l2,
    lsem,
    wosem,
    t1s,
    t1r,
    t2s,
    t2r,
    tss,
    tsr,
    xes,
    xer,
    r1s,
    r1r,
    b1s,
    b1r,
    wzs,
    wzr,
    wts,
    wtr,
    wfs,
    wfr,
    kzs,
    kzr,
    kxs,
    kxr,
    r2s,
    r2r,
    b2s,
    b2r,
    ozs,
    ozr,
    ots,
    otr,
    ofs,
    ofr,
    xfs,
    xfr,
    l1s,
    l1r,
    l2s,
    l2r,
):
    h = lax.axis_index("head")
    z = lax.axis_index("branch")
    s = lax.axis_index("seq")
    c = lax.rem(h, 2)
    y = lax.rem(lax.div(h, 2), YN)
    x = lax.div(h, 16)
    p = lax.rem(z, 2)
    nx = 1 - x
    np_ = 1 - p

    def yy(off):
        return lax.rem(y + off, YN)

    def rcopy(src, dst, ssem, rsem, dev):
        return pltpu.make_async_remote_copy(
            src_ref=src, dst_ref=dst, send_sem=ssem, recv_sem=rsem,
            device_id=dev, device_id_type=MESH,
        )

    sib = {"head": hid(x, y, 1 - c)}
    up = {"head": hid(x, yy(1), c)}
    down = {"head": hid(x, yy(7), c)}
    inner = {"head": hid(nx, y, c)}
    outer = {"head": hid(nx, y, c), "seq": 1 - s}
    far = {"seq": 1 - s}
    zpart = {"branch": z + 1 - 2 * p}

    cp_mod = pltpu.make_async_copy(mod_hbm.at[lax.div(z, 2)], modv, lsem.at[0])
    cp_wq = pltpu.make_async_copy(wq_hbm, wqv, lsem.at[1])
    cp_wkv = pltpu.make_async_copy(wkv_hbm, wkv2, lsem.at[2])
    cp_lat = pltpu.make_async_copy(lat_hbm, lat_ref, lsem.at[3])
    cp_noi = pltpu.make_async_copy(noi_hbm, noi_ref, lsem.at[4])
    cp_text = pltpu.make_async_copy(text_hbm, text_ref, lsem.at[5])
    cp_level = pltpu.make_async_copy(level_hbm, level_ref, lsem.at[6])
    cp_length = pltpu.make_async_copy(length_hbm, length_ref, lsem.at[7])
    cp_level.start()
    cp_lat.start()
    cp_noi.start()
    cp_text.start()
    cp_length.start()
    cp_wq.start()
    cp_mod.start()
    cp_wkv.start()

    def cp_wo(i):
        return pltpu.make_async_copy(
            wo_hbm.at[:, pl.ds(i * 256, 256)], wo.at[x, p, i], wosem.at[i]
        )

    for i in range(YN):
        cp_wo(i).start()

    barrier = pltpu.get_barrier_semaphore()
    peers = []
    for dz in range(ZN):
        for x2 in range(2):
            zt = lax.rem(z + dz, ZN)
            if dz == 0:
                if x2 == 0:
                    peers.append(inner)
            else:
                peers.append({"branch": zt, "head": hid(x2, y, c)})
    for off in range(1, YN):
        peers.append({"head": hid(x, yy(off), c)})
    peers.append(sib)
    peers.append({"head": hid(nx, y, 1 - c)})
    for xx in (x, nx):
        for cc in (c, 1 - c):
            peers.append({"head": hid(xx, y, cc), "seq": 1 - s})
    for dev in peers:
        pl.semaphore_signal(barrier, inc=1, device_id=dev, device_id_type=MESH)

    cp_level.wait()
    cp_length.wait()
    level_time = (level_ref[0].astype(F32) + 0.5) / LEVELS
    noise_level = 1.0 - (1.0 - sigma_min) * level_time
    mine = pl.ds(pl.multiple_of(x * TOK, TOK), TOK)
    theirs = pl.ds(pl.multiple_of(nx * TOK, TOK), TOK)

    def noisy_of(clean, noise):
        return (level_time * clean.astype(F32) + noise_level * noise.astype(F32)).astype(BF16)

    cp_lat.wait()
    cp_noi.wait()
    nz[h] = noisy_of(lat_ref[:, mine], noi_ref[:, mine])
    text_rows = pl.ds(pl.multiple_of(s * 16, 16), 16)
    my_rows = pl.ds(pl.multiple_of(z * 16, 16), 16)
    my_lanes = pl.ds(pl.multiple_of(c * 128, 128), 128)

    cp_text.wait()

    @pl.when(x == p)
    def _():
        tx[y, my_rows, my_lanes] = text_ref[text_rows, :]

    cp_wq.wait()

    def turn(i, carry):
        block = wqv[pl.ds(pl.multiple_of(i * 384, 384), 384), :]
        wq[x, p, i] = jnp.transpose(block.astype(F32)).astype(BF16)
        return carry

    lax.fori_loop(0, YN, turn, 0)

    pl.semaphore_wait(barrier, len(peers))

    def t1(j, x2):
        return rcopy(
            text_ref.at[text_rows, :], tx.at[y, my_rows, my_lanes],
            t1s.at[j, x2], t1r.at[z],
            {"branch": 2 * j + x, "head": hid(x2, y, c)},
        )

    def t1_remote(j, x2):
        return jnp.logical_or(2 * j + x != z, x2 != x)

    for j in range(4):
        for x2 in range(2):
            @pl.when(t1_remote(j, x2))
            def _(j=j, x2=x2):
                t1(j, x2).start()

    xe = [
        rcopy(lat_ref.at[:, theirs], nlat, xes.at[0], xer.at[0], inner),
        rcopy(noi_ref.at[:, theirs], nnoi, xes.at[1], xer.at[1], inner),
    ]

    def piece(buf, x2, y2):
        return buf.at[hid(x2, y2, c)]

    def ring(buf, ssem, rsem, x2, y2, way):
        at = piece(buf, x2, y2)
        return rcopy(at, at, ssem.at[x2, y2, way], rsem.at[x2, y2], up if way == 0 else down)

    def bridge(buf, ssem, rsem, x2, y2):
        at = piece(buf, x2, y2)
        return rcopy(at, at, ssem.at[x2, y2], rsem.at[x2, y2], sib)

    def launch(buf, rs, rr, bs, br, x2):
        ring(buf, rs, rr, x2, y, 0).start()
        ring(buf, rs, rr, x2, y, 1).start()
        bridge(buf, bs, br, x2, y).start()

    launch(nz, r1s, r1r, b1s, b1r, x)
    for copy in xe:
        copy.start()

    def w_z(buf, ssem, rsem, i):
        at = buf.at[x, p, i]
        return rcopy(at, at, ssem.at[i], rsem.at[i], zpart)

    def w_out(buf, ssem, rsem, i):
        at = buf.at[x, p, i]
        return rcopy(at, at, ssem.at[i], rsem.at[i], outer)

    def w_fwd(buf, ssem, rsem, i):
        at = buf.at[x, np_, i]
        return rcopy(at, at, ssem.at[i], rsem.at[i], inner)

    for off in ORDER:
        if off != 4:
            w_z(wq, wzs, wzr, yy(off)).start()
        w_out(wq, wts, wtr, yy(off)).start()

    cp_mod.wait()
    pick = (lax.broadcasted_iota(jnp.int32, (LEVELS, 1), 0) == level_ref[0]).astype(F32)
    for k in range(3):
        for i in range(16):
            row = jnp.sum(
                modv[k, :, i * 384 : (i + 1) * 384].astype(F32) * pick, axis=0, keepdims=True
            )
            rows[k, i] = row + 1.0 if k == 1 else row
    for x2 in range(2):
        gate = jnp.broadcast_to(rows[2, x2 * 8 + y], (128, 384))
        gcol[x2] = jnp.transpose(gate)

    def t1_wait(zs):
        rcopy(
            text_ref.at[text_rows, :],
            tx.at[y, pl.ds(zs * 16, 16), my_lanes],
            t1s.at[0, 0], t1r.at[zs], inner,
        ).wait_recv()

    def t2(off):
        at = tx.at[y, :, my_lanes]
        return rcopy(at, at, t2s.at[off], t2r.at[y], {"head": hid(x, yy(off), c)})

    def t2_wait(y2):
        at = tx.at[y2, :, my_lanes]
        rcopy(at, at, t2s.at[0], t2r.at[y2], sib).wait_recv()

    def t_sib(y2):
        at = tx.at[y2, :, my_lanes]
        return rcopy(at, at, tss.at[y2], tsr.at[y2], sib)

    def t_sib_wait(y2):
        at = tx.at[y2, :, pl.ds(pl.multiple_of((1 - c) * 128, 128), 128)]
        rcopy(at, at, tss.at[y2], tsr.at[y2], sib).wait_recv()

    pacc[...] = jnp.zeros_like(pacc)
    uacc[...] = jnp.zeros_like(uacc)
    vacc[...] = jnp.zeros_like(vacc)
    s1acc[...] = jnp.zeros_like(s1acc)
    s2acc[...] = jnp.zeros_like(s2acc)

    def project(x2, y2):
        chip = x2 * 8 + y2
        n = nz[pl.ds(hid(x2, y2, 0), 2)].reshape(384, TOK)
        scale = rows[1, chip]
        shift = rows[0, chip]
        for g in range(2):
            w = wq[g, x2, y2].astype(F32)
            ws = w * scale
            high = ws.astype(BF16)
            low = (ws - high.astype(F32)).astype(BF16)
            pacc[g] += jnp.dot(high, n, preferred_element_type=F32) + jnp.dot(
                low, n, preferred_element_type=F32
            )
            uacc[g] += ws[:, 0:128] + ws[:, 128:256] + ws[:, 256:384]
            sh = w * shift
            vacc[g] += sh[:, 0:128] + sh[:, 128:256] + sh[:, 256:384]
        nf = n.astype(F32).reshape(48, 8, TOK)
        s1acc[...] += jnp.sum(nf, axis=0)
        s2acc[...] += jnp.sum(nf * nf, axis=0)

    def ring_step(buf, rs, rr, bs, br, x2, rises, k):
        for way in range(2):
            last = rises if way == 0 else not rises
            y2 = yy(8 - k) if way == 0 else yy(k)
            if k < 4 or last:
                ring(buf, rs, rr, x2, y2, way).wait_recv()
                if k < 3 or (k == 3 and last):
                    ring(buf, rs, rr, x2, y2, way).start()
                bridge(buf, bs, br, x2, y2).start()

    def bridge_wait(buf, bs, br, y2):
        for x2 in range(2):
            at = buf.at[hid(x2, y2, 1 - c)]
            rcopy(at, at, bs.at[x2, y2], br.at[x2, y2], sib).wait_recv()

    def fwd_wait(buf, fs, fr, i):
        at = buf.at[nx, np_, i]
        rcopy(at, at, fs.at[i], fr.at[i], inner).wait_recv()

    def out_wait(buf, os_, or_, i):
        at = buf.at[nx, p, i]
        rcopy(at, at, os_.at[i], or_.at[i], outer).wait_recv()

    def z_forward(buf, zs, zr, fs, fr, i):
        at = buf.at[x, np_, i]
        rcopy(at, at, zs.at[i], zr.at[i], zpart).wait_recv()
        w_fwd(buf, fs, fr, i).start()

    def offsets(k):
        return (k,) if k in (0, 4) else (k, 8 - k)

    def query_block(k):
        for off in offsets(k):
            i = yy(off)
            bridge_wait(nz, b1s, b1r, i)
            out_wait(wq, wts, wtr, i)
            project(p, i)
            fwd_wait(wq, wfs, wfr, i)
            project(np_, i)

    def wq_forward(j):
        z_forward(wq, wzs, wzr, wfs, wfr, yy(ORDER[j]))

    def wo_forward(j):
        z_forward(wo, ozs, ozr, ofs, ofr, yy(ORDER[j]))

    def own_step(k):
        ring_step(nz, r1s, r1r, b1s, b1r, x, True, k)

    def next_step(k):
        ring_step(nz, r1s, r1r, b1s, b1r, nx, False, k)

    own_step(1)
    wq_forward(0)
    for copy in xe:
        copy.wait_recv()
    nz[hid(nx, y, c)] = noisy_of(nlat[...], nnoi[...])
    launch(nz, r1s, r1r, b1s, b1r, nx)
    for zs in range(ZN):
        @pl.when(jnp.logical_or(x != p, z != zs))
        def _(zs=zs):
            t1_wait(zs)
    for off in (4, 3, 5, 2, 6, 1, 7):
        t2(off).start()
    t_sib(y).start()
    wq_forward(1)
    own_step(2)
    wq_forward(2)

    cp_wkv.wait()

    def spread(i, carry):
        at = pl.ds(pl.multiple_of(i * 512, 512), 512)
        wkvf[...] = wkv2[at, :].astype(F32)
        to = pl.ds(pl.multiple_of(i * 256, 256), 256)
        wkv[to, 0:128] = wkvf[pl.ds(0, 256, stride=2), :].astype(BF16)
        wkv[to, 128:256] = wkvf[pl.ds(1, 256, stride=2), :].astype(BF16)
        return carry

    lax.fori_loop(0, YN, spread, 0)

    next_step(1)
    wq_forward(3)
    for off in (1, 7, 2, 6, 3, 5, 4):
        t2_wait(yy(off))
        t_sib(yy(off)).start()
    wq_forward(4)
    own_step(3)
    for y2 in range(YN):
        t_sib_wait(y2)

    kvs[0:128, :] = jnp.zeros((128, 256), F32)
    squares = jnp.zeros((128, 256), F32)
    for y2 in range(YN):
        t = tx[y2]
        kvs[0:128, :] += jnp.dot(
            t, wkv[y2 * 256 : (y2 + 1) * 256, :], preferred_element_type=F32
        )
        tf = t.astype(F32)
        squares = squares + tf * tf
    square_col = jnp.sum(squares, axis=1, keepdims=True)
    square_row = jnp.transpose(jnp.broadcast_to(square_col, (128, 128)))[0:8]
    kvs[128:136, 0:128] = square_row
    kvs[128:136, 128:256] = square_row
    kz = rcopy(kvs, kvr, kzs, kzr, zpart)
    kz.start()

    for i in range(YN):
        cp_wo(i).wait()
    w_z(wq, wzs, wzr, yy(4)).start()
    for off in ORDER:
        w_z(wo, ozs, ozr, yy(off)).start()
    w_out(wo, ots, otr, yy(ORDER[0])).start()

    wq_forward(5)
    next_step(2)
    wq_forward(6)
    query_block(0)
    query_block(1)
    own_step(4)

    kz.wait_recv()
    other_col = jnp.transpose(jnp.broadcast_to(kvr[128:129, 0:128], (128, 128)))[:, 0:1]
    text_rstd = lax.rsqrt((square_col + other_col) / TD + epsilon)
    text_proj = (kvs[0:128, :] + kvr[0:128, :]) * text_rstd
    keys = text_proj[:, 0:128]
    keys = keys * lax.rsqrt(jnp.mean(keys * keys, axis=1, keepdims=True) + epsilon)
    kvb[x, s, 0] = keys.astype(BF16)
    kvb[x, s, 1] = jnp.transpose(text_proj[:, 128:256]).astype(BF16)
    kx = [
        rcopy(kvb.at[x, s], kvb.at[x, s], kxs.at[k], kxr.at[x, s], dev)
        for k, dev in enumerate((inner, far, outer))
    ]
    for copy in kx:
        copy.start()

    for off in ORDER[1:]:
        w_out(wo, ots, otr, yy(off)).start()
    next_step(3)
    wq_forward(7)
    query_block(2)
    next_step(4)
    wo_forward(0)
    query_block(3)
    query_block(4)

    for x2, s2 in ((nx, s), (x, 1 - s), (nx, 1 - s)):
        at = kvb.at[x2, s2]
        rcopy(at, at, kxs.at[0], kxr.at[x2, s2], inner).wait_recv()
    mean_row = jnp.sum(s1acc[...], axis=0, keepdims=True) / D
    var_row = jnp.sum(s2acc[...], axis=0, keepdims=True) / D - mean_row * mean_row
    rstd = lax.rsqrt(var_row + epsilon)
    index = lax.broadcasted_iota(jnp.int32, (128, TOK), 0)
    position = lax.div(index, 16) * 32 + lax.rem(index, 16)
    for g in range(2):
        u = jnp.sum(uacc[g], axis=1, keepdims=True)
        v = jnp.sum(vacc[g], axis=1, keepdims=True)
        q = (pacc[g] - u * mean_row) * rstd + v
        q = (q * lax.rsqrt(jnp.mean(q * q, axis=0, keepdims=True) + epsilon)).astype(BF16)
        exps = []
        for s2 in range(2):
            scores = jnp.dot(kvb[g, s2, 0], q, preferred_element_type=F32) / jnp.sqrt(F32(HD))
            live = position + 16 * s2 < length_ref[0]
            exps.append(jnp.where(live, jnp.exp(scores), 0.0))
        total = jnp.sum(exps[0], axis=0, keepdims=True) + jnp.sum(exps[1], axis=0, keepdims=True)
        inverse = 1.0 / total
        mixed = jnp.dot(
            kvb[g, 0, 1], (exps[0] * inverse).astype(BF16), preferred_element_type=F32
        ) + jnp.dot(kvb[g, 1, 1], (exps[1] * inverse).astype(BF16), preferred_element_type=F32)
        att[hid(g, y, c)] = mixed.astype(BF16)
        launch(att, r2s, r2r, b2s, b2r, g)
        wo_forward(1 + g)

    oacc[...] = jnp.zeros_like(oacc)

    def out_project(x2, y2):
        a = att[pl.ds(hid(x2, y2, 0), 2)].reshape(256, TOK)
        for g in range(2):
            oacc[g] += jnp.dot(wo[g, x2, y2], a, preferred_element_type=F32)

    def out_block(k):
        for off in offsets(k):
            i = yy(off)
            bridge_wait(att, b2s, b2r, i)
            out_wait(wo, ots, otr, i)
            out_project(p, i)
            fwd_wait(wo, ofs, ofr, i)
            out_project(np_, i)

    def att_step(g, k):
        ring_step(att, r2s, r2r, b2s, b2r, g, g == 0, k)

    att_step(0, 1)
    wo_forward(3)
    att_step(1, 1)
    out_block(0)
    att_step(0, 2)
    wo_forward(4)
    att_step(1, 2)
    out_block(1)
    wo_forward(5)
    att_step(0, 3)
    wo_forward(6)
    att_step(1, 3)
    out_block(2)
    att_step(0, 4)
    wo_forward(7)
    att_step(1, 4)
    out_block(3)
    out_block(4)

    half = pl.ds(pl.multiple_of(c * CH, CH), CH)

    def denoise(x2):
        gate = gcol[x2, half, :]
        gated = oacc[x2] * jnp.concatenate([gate, gate], axis=1)
        return (nz[hid(x2, y, c)].astype(F32) + gated).astype(BF16)

    def error_of(done, clean, noise):
        target = clean.astype(F32) - (1.0 - sigma_min) * noise.astype(F32)
        e = done.astype(F32) - target
        e = e * e
        e = jnp.sum(e.reshape(CH // 8, 8, TOK), axis=0)
        return e[:, 0:128] + e[:, 128:256]

    done = denoise(nx)
    xs2[...] = done
    error = error_of(done, nlat[...], nnoi[...])
    done = denoise(x)
    out_ref[:, mine] = done
    error = error + error_of(done, lat_ref[:, mine], noi_ref[:, mine])

    def slot(ss, xx, cc):
        return ss * 4 + xx * 2 + cc

    here = slot(s, x, c)
    l1[here] = error
    group = []
    for ds in range(2):
        for dx in range(2):
            for dc in range(2):
                if ds + dx + dc:
                    s2 = s if ds == 0 else 1 - s
                    x2 = x if dx == 0 else nx
                    c2 = c if dc == 0 else 1 - c
                    group.append((s2, x2, c2))
    for k, (s2, x2, c2) in enumerate(group):
        rcopy(
            l1.at[here], l1.at[here], l1s.at[k], l1r.at[here], {"head": hid(x2, y, c2), "seq": s2}
        ).start()
    xf = rcopy(xs2, xr2, xfs, xfr, inner)
    xf.start()
    for s2, x2, c2 in group:
        at = l1.at[slot(s2, x2, c2)]
        rcopy(at, at, l1s.at[0], l1r.at[slot(s2, x2, c2)], sib).wait_recv()
    l2[y] = jnp.sum(l1[...], axis=0)
    for off in range(1, YN):
        rcopy(
            l2.at[y], l2.at[y], l2s.at[off], l2r.at[y], {"head": hid(x, yy(off), c)}
        ).start()

    for j in range(4):
        for x2 in range(2):
            @pl.when(t1_remote(j, x2))
            def _(j=j, x2=x2):
                t1(j, x2).wait_send()
    xf.wait_recv()
    out_ref[:, theirs] = xr2[...]
    for copy in xe:
        copy.wait_send()
    for off in range(1, YN):
        t2(off).wait_send()
    kz.wait_send()
    for copy in kx:
        copy.wait_send()
    xf.wait_send()

    for i in range(YN):
        t_sib(i).wait_send()
        w_z(wq, wzs, wzr, i).wait_send()
        w_out(wq, wts, wtr, i).wait_send()
        w_fwd(wq, wfs, wfr, i).wait_send()
        w_z(wo, ozs, ozr, i).wait_send()
        w_out(wo, ots, otr, i).wait_send()
        w_fwd(wo, ofs, ofr, i).wait_send()
        for x2 in range(2):
            bridge(nz, b1s, b1r, x2, i).wait_send()
            bridge(att, b2s, b2r, x2, i).wait_send()
    for buf, rs, rr in ((nz, r1s, r1r), (att, r2s, r2r)):
        for x2 in range(2):
            rises = x2 == 0
            at = x2 if buf is att else (x if rises else nx)
            for k in range(4):
                if k < 3 or rises:
                    ring(buf, rs, rr, at, yy(8 - k), 0).wait_send()
                if k < 3 or not rises:
                    ring(buf, rs, rr, at, yy(k), 1).wait_send()
    for k, (s2, x2, c2) in enumerate(group):
        rcopy(l1.at[here], l1.at[here], l1s.at[k], l1r.at[here], sib).wait_send()

    for off in range(1, YN):
        at = l2.at[yy(off)]
        rcopy(at, at, l2s.at[off], l2r.at[yy(off)], sib).wait_recv()
    for off in range(1, YN):
        rcopy(l2.at[y], l2.at[y], l2s.at[off], l2r.at[y], sib).wait_send()
    loss_ref[0] = jnp.sum(jnp.sum(l2[...], axis=0)) / (1024 * D)


def local(
    text_hidden, text_length, latent, noise, level_index, mod_table, wq_halves, wo_halves, wkv_halves
):
    dma = pltpu.SemaphoreType.DMA
    vmem = pltpu.VMEM
    any_ = pl.BlockSpec(memory_space=pl.ANY)
    in_vmem = pl.BlockSpec(memory_space=pltpu.VMEM)
    in_smem = pl.BlockSpec(memory_space=pltpu.SMEM)
    in_hbm = pl.BlockSpec(memory_space=pltpu.HBM)
    out, loss = pl.pallas_call(
        kernel,
        out_shape=(
            jax.ShapeDtypeStruct((CH, 2 * TOK), BF16),
            jax.ShapeDtypeStruct((1,), F32),
        ),
        in_specs=[in_hbm] * 2 + [any_] * 7,
        out_specs=(in_vmem, in_smem),
        scratch_shapes=[
            pltpu.SMEM((1,), jnp.int32),
            pltpu.SMEM((1,), jnp.int32),
            vmem((32, 128), BF16),
            vmem((CH, 2 * TOK), BF16),
            vmem((CH, 2 * TOK), BF16),
            vmem((3, LEVELS, D), BF16),
            vmem((D // 2, HD), BF16),
            vmem((TD, HD), BF16),
            vmem((512, HD), F32),
            vmem((TD // 2, 256), BF16),
            vmem((2, 2, YN, CH, 256), BF16),
            vmem((2, 2, YN, HD, 384), BF16),
            vmem((32, CH, TOK), BF16),
            vmem((CH, TOK), BF16),
            vmem((CH, TOK), BF16),
            vmem((3, 16, 1, 384), F32),
            vmem((2, 384, 128), F32),
            vmem((YN, 128, 256), BF16),
            vmem((136, 256), F32),
            vmem((136, 256), F32),
            vmem((2, 2, 2, 128, 128), BF16),
            vmem((2, HD, TOK), F32),
            vmem((2, HD, 128), F32),
            vmem((2, HD, 128), F32),
            vmem((8, TOK), F32),
            vmem((8, TOK), F32),
            vmem((32, HD, TOK), BF16),
            vmem((2, CH, TOK), F32),
            vmem((CH, TOK), BF16),
            vmem((CH, TOK), BF16),
            vmem((8, 8, 128), F32),
            vmem((YN, 8, 128), F32),
            dma((8,)),
            dma((YN,)),
            dma((4, 2)),
            dma((ZN,)),
            dma((YN,)),
            dma((YN,)),
            dma((YN,)),
            dma((YN,)),
            dma((2,)),
            dma((2,)),
            dma((2, YN, 2)),
            dma((2, YN)),
            dma((2, YN)),
            dma((2, YN)),
            dma((YN,)),
            dma((YN,)),
            dma((YN,)),
            dma((YN,)),
            dma((YN,)),
            dma((YN,)),
            dma,
            dma,
            dma((3,)),
            dma((2, 2)),
            dma((2, YN, 2)),
            dma((2, YN)),
            dma((2, YN)),
            dma((2, YN)),
            dma((YN,)),
            dma((YN,)),
            dma((YN,)),
            dma((YN,)),
            dma((YN,)),
            dma((YN,)),
            dma,
            dma,
            dma((7,)),
            dma((8,)),
            dma((YN,)),
            dma((YN,)),
        ],
        compiler_params=pltpu.CompilerParams(
            collective_id=0, has_side_effects=True, vmem_limit_bytes=60 << 20
        ),
    )(
        level_index,
        text_length,
        text_hidden,
        jnp.swapaxes(latent[0], 0, 1),
        jnp.swapaxes(noise[0], 0, 1),
        jnp.swapaxes(mod_table, 1, 2),
        wq_halves[0],
        jnp.swapaxes(wo_halves[0], 0, 1),
        wkv_halves[0].reshape(TD, HD),
    )
    return (jnp.swapaxes(out, 0, 1)[None], loss)


def solution(mesh):
    return jax.shard_map(
        local,
        mesh=mesh,
        in_specs=(
            P("branch", "head"),
            P(),
            P("branch", "seq", "head"),
            P("branch", "seq", "head"),
            P("branch"),
            P(),
            P("branch", None, "head"),
            P("branch", None, "head"),
            P("branch", None, None, "head"),
        ),
        out_specs=(P("branch", "seq", "head"), P("branch")),
        check_vma=False,
    )
```

```python
import jax
import jax.numpy as jnp
from jax import lax
from jax.experimental import pallas as pl
from jax.experimental.pallas import tpu as pltpu
from jax.sharding import PartitionSpec as P

MESH = pl.DeviceIdType.MESH
F32 = jnp.float32
BF16 = jnp.bfloat16

D = 6144
TD = 4096
HD = 128
LEVELS = 8
YN = 8
ZN = 8
CH = 192
TOK = 256
epsilon = 1e-06
sigma_min = 1e-05

ORDER = (0, 1, 7, 2, 6, 3, 5, 4)


def hid(x, y, c):
    return x * 16 + y * 2 + c


def kernel(
    level_hbm,
    length_hbm,
    text_hbm,
    lat_hbm,
    noi_hbm,
    mod_hbm,
    wq_hbm,
    wo_hbm,
    wkv_hbm,
    out_ref,
    loss_ref,
    level_ref,
    length_ref,
    text_ref,
    lat_ref,
    noi_ref,
    modv,
    wqv,
    wkv2,
    wkvf,
    wkv,
    wo,
    wq,
    nz,
    nlat,
    nnoi,
    rows,
    gcol,
    tx,
    kvs,
    kvr,
    kvb,
    pacc,
    uacc,
    vacc,
    s1acc,
    s2acc,
    att,
    oacc,
    xs2,
    xr2,
    l1,
    l2,
    lsem,
    wosem,
    t1s,
    t1r,
    t2s,
    t2r,
    tss,
    tsr,
    xes,
    xer,
    r1s,
    r1r,
    b1s,
    b1r,
    wzs,
    wzr,
    wts,
    wtr,
    wfs,
    wfr,
    kzs,
    kzr,
    kxs,
    kxr,
    r2s,
    r2r,
    b2s,
    b2r,
    ozs,
    ozr,
    ots,
    otr,
    ofs,
    ofr,
    xfs,
    xfr,
    l1s,
    l1r,
    l2s,
    l2r,
):
    h = lax.axis_index("head")
    z = lax.axis_index("branch")
    s = lax.axis_index("seq")
    c = lax.rem(h, 2)
    y = lax.rem(lax.div(h, 2), YN)
    x = lax.div(h, 16)
    p = lax.rem(z, 2)
    nx = 1 - x
    np_ = 1 - p

    def yy(off):
        return lax.rem(y + off, YN)

    def rcopy(src, dst, ssem, rsem, dev):
        return pltpu.make_async_remote_copy(
            src_ref=src, dst_ref=dst, send_sem=ssem, recv_sem=rsem,
            device_id=dev, device_id_type=MESH,
        )

    sib = {"head": hid(x, y, 1 - c)}
    up = {"head": hid(x, yy(1), c)}
    down = {"head": hid(x, yy(7), c)}
    inner = {"head": hid(nx, y, c)}
    outer = {"head": hid(nx, y, c), "seq": 1 - s}
    far = {"seq": 1 - s}
    zpart = {"branch": z + 1 - 2 * p}

    cp_mod = pltpu.make_async_copy(mod_hbm.at[lax.div(z, 2)], modv, lsem.at[0])
    cp_wq = pltpu.make_async_copy(wq_hbm, wqv, lsem.at[1])
    cp_wkv = pltpu.make_async_copy(wkv_hbm, wkv2, lsem.at[2])
    cp_lat = pltpu.make_async_copy(lat_hbm, lat_ref, lsem.at[3])
    cp_noi = pltpu.make_async_copy(noi_hbm, noi_ref, lsem.at[4])
    cp_text = pltpu.make_async_copy(text_hbm, text_ref, lsem.at[5])
    cp_level = pltpu.make_async_copy(level_hbm, level_ref, lsem.at[6])
    cp_length = pltpu.make_async_copy(length_hbm, length_ref, lsem.at[7])
    cp_level.start()
    cp_lat.start()
    cp_noi.start()
    cp_text.start()
    cp_length.start()
    cp_wq.start()
    cp_mod.start()
    cp_wkv.start()

    def cp_wo(i):
        return pltpu.make_async_copy(
            wo_hbm.at[:, pl.ds(i * 256, 256)], wo.at[x, p, i], wosem.at[i]
        )

    for i in range(YN):
        cp_wo(i).start()

    barrier = pltpu.get_barrier_semaphore()
    peers = []
    for dz in range(ZN):
        for x2 in range(2):
            zt = lax.rem(z + dz, ZN)
            if dz == 0:
                if x2 == 0:
                    peers.append(inner)
            else:
                peers.append({"branch": zt, "head": hid(x2, y, c)})
    for off in range(1, YN):
        peers.append({"head": hid(x, yy(off), c)})
    peers.append(sib)
    peers.append({"head": hid(nx, y, 1 - c)})
    for xx in (x, nx):
        for cc in (c, 1 - c):
            peers.append({"head": hid(xx, y, cc), "seq": 1 - s})
    for dev in peers:
        pl.semaphore_signal(barrier, inc=1, device_id=dev, device_id_type=MESH)

    cp_level.wait()
    cp_length.wait()
    level_time = (level_ref[0].astype(F32) + 0.5) / LEVELS
    noise_level = 1.0 - (1.0 - sigma_min) * level_time
    mine = pl.ds(pl.multiple_of(x * TOK, TOK), TOK)
    theirs = pl.ds(pl.multiple_of(nx * TOK, TOK), TOK)

    def noisy_of(clean, noise):
        return (level_time * clean.astype(F32) + noise_level * noise.astype(F32)).astype(BF16)

    cp_lat.wait()
    cp_noi.wait()
    nz[h] = noisy_of(lat_ref[:, mine], noi_ref[:, mine])
    text_rows = pl.ds(pl.multiple_of(s * 16, 16), 16)
    my_rows = pl.ds(pl.multiple_of(z * 16, 16), 16)
    my_lanes = pl.ds(pl.multiple_of(c * 128, 128), 128)

    cp_text.wait()

    @pl.when(x == p)
    def _():
        tx[y, my_rows, my_lanes] = text_ref[text_rows, :]

    cp_wq.wait()

    def turn(i, carry):
        block = wqv[pl.ds(pl.multiple_of(i * 384, 384), 384), :]
        wq[x, p, i] = jnp.transpose(block.astype(F32)).astype(BF16)
        return carry

    lax.fori_loop(0, YN, turn, 0)

    pl.semaphore_wait(barrier, len(peers))

    def t1(j, x2):
        return rcopy(
            text_ref.at[text_rows, :], tx.at[y, my_rows, my_lanes],
            t1s.at[j, x2], t1r.at[z],
            {"branch": 2 * j + x, "head": hid(x2, y, c)},
        )

    def t1_remote(j, x2):
        return jnp.logical_or(2 * j + x != z, x2 != x)

    for j in range(4):
        for x2 in range(2):
            @pl.when(t1_remote(j, x2))
            def _(j=j, x2=x2):
                t1(j, x2).start()

    xe = [
        rcopy(lat_ref.at[:, theirs], nlat, xes.at[0], xer.at[0], inner),
        rcopy(noi_ref.at[:, theirs], nnoi, xes.at[1], xer.at[1], inner),
    ]

    def piece(buf, x2, y2):
        return buf.at[hid(x2, y2, c)]

    def ring(buf, ssem, rsem, x2, y2, way):
        at = piece(buf, x2, y2)
        return rcopy(at, at, ssem.at[x2, y2, way], rsem.at[x2, y2], up if way == 0 else down)

    def bridge(buf, ssem, rsem, x2, y2):
        at = piece(buf, x2, y2)
        return rcopy(at, at, ssem.at[x2, y2], rsem.at[x2, y2], sib)

    def launch(buf, rs, rr, bs, br, x2):
        ring(buf, rs, rr, x2, y, 0).start()
        ring(buf, rs, rr, x2, y, 1).start()
        bridge(buf, bs, br, x2, y).start()

    launch(nz, r1s, r1r, b1s, b1r, x)
    for copy in xe:
        copy.start()

    def w_z(buf, ssem, rsem, i):
        at = buf.at[x, p, i]
        return rcopy(at, at, ssem.at[i], rsem.at[i], zpart)

    def w_out(buf, ssem, rsem, i):
        at = buf.at[x, p, i]
        return rcopy(at, at, ssem.at[i], rsem.at[i], outer)

    def w_fwd(buf, ssem, rsem, i):
        at = buf.at[x, np_, i]
        return rcopy(at, at, ssem.at[i], rsem.at[i], inner)

    for off in ORDER:
        w_z(wq, wzs, wzr, yy(off)).start()
        w_out(wq, wts, wtr, yy(off)).start()

    cp_mod.wait()
    pick = (lax.broadcasted_iota(jnp.int32, (LEVELS, 1), 0) == level_ref[0]).astype(F32)
    for k in range(3):
        for i in range(16):
            row = jnp.sum(
                modv[k, :, i * 384 : (i + 1) * 384].astype(F32) * pick, axis=0, keepdims=True
            )
            rows[k, i] = row + 1.0 if k == 1 else row
    for x2 in range(2):
        gate = jnp.broadcast_to(rows[2, x2 * 8 + y], (128, 384))
        gcol[x2] = jnp.transpose(gate)

    def t1_wait(zs):
        rcopy(
            text_ref.at[text_rows, :],
            tx.at[y, pl.ds(zs * 16, 16), my_lanes],
            t1s.at[0, 0], t1r.at[zs], inner,
        ).wait_recv()

    def t2(off):
        at = tx.at[y, :, my_lanes]
        return rcopy(at, at, t2s.at[off], t2r.at[y], {"head": hid(x, yy(off), c)})

    def t2_wait(y2):
        at = tx.at[y2, :, my_lanes]
        rcopy(at, at, t2s.at[0], t2r.at[y2], sib).wait_recv()

    def t_sib(y2):
        at = tx.at[y2, :, my_lanes]
        return rcopy(at, at, tss.at[y2], tsr.at[y2], sib)

    def t_sib_wait(y2):
        at = tx.at[y2, :, pl.ds(pl.multiple_of((1 - c) * 128, 128), 128)]
        rcopy(at, at, tss.at[y2], tsr.at[y2], sib).wait_recv()

    pacc[...] = jnp.zeros_like(pacc)
    uacc[...] = jnp.zeros_like(uacc)
    vacc[...] = jnp.zeros_like(vacc)
    s1acc[...] = jnp.zeros_like(s1acc)
    s2acc[...] = jnp.zeros_like(s2acc)

    def project(x2, y2):
        chip = x2 * 8 + y2
        n = nz[pl.ds(hid(x2, y2, 0), 2)].reshape(384, TOK)
        scale = rows[1, chip]
        shift = rows[0, chip]
        for g in range(2):
            w = wq[g, x2, y2].astype(F32)
            ws = w * scale
            high = ws.astype(BF16)
            low = (ws - high.astype(F32)).astype(BF16)
            pacc[g] += jnp.dot(high, n, preferred_element_type=F32) + jnp.dot(
                low, n, preferred_element_type=F32
            )
            uacc[g] += ws[:, 0:128] + ws[:, 128:256] + ws[:, 256:384]
            sh = w * shift
            vacc[g] += sh[:, 0:128] + sh[:, 128:256] + sh[:, 256:384]
        nf = n.astype(F32).reshape(48, 8, TOK)
        s1acc[...] += jnp.sum(nf, axis=0)
        s2acc[...] += jnp.sum(nf * nf, axis=0)

    def ring_step(buf, rs, rr, bs, br, x2, rises, k):
        for way in range(2):
            last = rises if way == 0 else not rises
            y2 = yy(8 - k) if way == 0 else yy(k)
            if k < 4 or last:
                ring(buf, rs, rr, x2, y2, way).wait_recv()
                if k < 3 or (k == 3 and last):
                    ring(buf, rs, rr, x2, y2, way).start()
                bridge(buf, bs, br, x2, y2).start()

    def bridge_wait(buf, bs, br, y2):
        for x2 in range(2):
            at = buf.at[hid(x2, y2, 1 - c)]
            rcopy(at, at, bs.at[x2, y2], br.at[x2, y2], sib).wait_recv()

    def fwd_wait(buf, fs, fr, i):
        at = buf.at[nx, np_, i]
        rcopy(at, at, fs.at[i], fr.at[i], inner).wait_recv()

    def out_wait(buf, os_, or_, i):
        at = buf.at[nx, p, i]
        rcopy(at, at, os_.at[i], or_.at[i], outer).wait_recv()

    def z_forward(buf, zs, zr, fs, fr, i):
        at = buf.at[x, np_, i]
        rcopy(at, at, zs.at[i], zr.at[i], zpart).wait_recv()
        w_fwd(buf, fs, fr, i).start()

    def offsets(k):
        return (k,) if k in (0, 4) else (k, 8 - k)

    def query_block(k):
        for off in offsets(k):
            i = yy(off)
            bridge_wait(nz, b1s, b1r, i)
            out_wait(wq, wts, wtr, i)
            project(p, i)
            fwd_wait(wq, wfs, wfr, i)
            project(np_, i)

    def wq_forward(j):
        z_forward(wq, wzs, wzr, wfs, wfr, yy(ORDER[j]))

    def wo_forward(j):
        z_forward(wo, ozs, ozr, ofs, ofr, yy(ORDER[j]))

    def own_step(k):
        ring_step(nz, r1s, r1r, b1s, b1r, x, True, k)

    def next_step(k):
        ring_step(nz, r1s, r1r, b1s, b1r, nx, False, k)

    own_step(1)
    wq_forward(0)
    for zs in range(ZN):
        @pl.when(jnp.logical_or(x != p, z != zs))
        def _(zs=zs):
            t1_wait(zs)
    for off in (4, 3, 5, 2, 6, 1, 7):
        t2(off).start()
    t_sib(y).start()
    for copy in xe:
        copy.wait_recv()
    nz[hid(nx, y, c)] = noisy_of(nlat[...], nnoi[...])
    launch(nz, r1s, r1r, b1s, b1r, nx)
    wq_forward(1)
    own_step(2)
    wq_forward(2)

    cp_wkv.wait()

    def spread(i, carry):
        at = pl.ds(pl.multiple_of(i * 512, 512), 512)
        wkvf[...] = wkv2[at, :].astype(F32)
        to = pl.ds(pl.multiple_of(i * 256, 256), 256)
        wkv[to, 0:128] = wkvf[pl.ds(0, 256, stride=2), :].astype(BF16)
        wkv[to, 128:256] = wkvf[pl.ds(1, 256, stride=2), :].astype(BF16)
        return carry

    lax.fori_loop(0, YN, spread, 0)

    next_step(1)
    wq_forward(3)
    for off in (1, 7, 2, 6, 3, 5, 4):
        t2_wait(yy(off))
        t_sib(yy(off)).start()
    wq_forward(4)

    kvs[0:128, :] = jnp.zeros((128, 256), F32)
    squares = jnp.zeros((128, 256), F32)
    for off in ORDER:
        y2 = yy(off)
        t_sib_wait(y2)
        t = tx[y2]
        kvs[0:128, :] += jnp.dot(
            t, wkv[pl.ds(pl.multiple_of(y2 * 256, 256), 256), :], preferred_element_type=F32
        )
        tf = t.astype(F32)
        squares = squares + tf * tf
    square_col = jnp.sum(squares, axis=1, keepdims=True)
    square_row = jnp.transpose(jnp.broadcast_to(square_col, (128, 128)))[0:8]
    kvs[128:136, 0:128] = square_row
    kvs[128:136, 128:256] = square_row
    kz = rcopy(kvs, kvr, kzs, kzr, zpart)
    kz.start()

    for i in range(YN):
        cp_wo(i).wait()
    for off in ORDER:
        w_z(wo, ozs, ozr, yy(off)).start()
    w_out(wo, ots, otr, yy(ORDER[0])).start()

    own_step(3)
    wq_forward(5)
    next_step(2)
    wq_forward(6)
    query_block(0)
    query_block(1)

    kz.wait_recv()
    other_col = jnp.transpose(jnp.broadcast_to(kvr[128:129, 0:128], (128, 128)))[:, 0:1]
    text_rstd = lax.rsqrt((square_col + other_col) / TD + epsilon)
    text_proj = (kvs[0:128, :] + kvr[0:128, :]) * text_rstd
    keys = text_proj[:, 0:128]
    keys = keys * lax.rsqrt(jnp.mean(keys * keys, axis=1, keepdims=True) + epsilon)
    kvb[x, s, 0] = keys.astype(BF16)
    kvb[x, s, 1] = jnp.transpose(text_proj[:, 128:256]).astype(BF16)
    kx = [
        rcopy(kvb.at[x, s], kvb.at[x, s], kxs.at[k], kxr.at[x, s], dev)
        for k, dev in enumerate((inner, far, outer))
    ]
    for copy in kx:
        copy.start()

    for off in ORDER[1:]:
        w_out(wo, ots, otr, yy(off)).start()
    own_step(4)
    next_step(3)
    wq_forward(7)
    query_block(2)
    query_block(3)
    next_step(4)
    wo_forward(0)
    query_block(4)

    for x2, s2 in ((nx, s), (x, 1 - s), (nx, 1 - s)):
        at = kvb.at[x2, s2]
        rcopy(at, at, kxs.at[0], kxr.at[x2, s2], inner).wait_recv()
    mean_row = jnp.sum(s1acc[...], axis=0, keepdims=True) / D
    var_row = jnp.sum(s2acc[...], axis=0, keepdims=True) / D - mean_row * mean_row
    rstd = lax.rsqrt(var_row + epsilon)
    index = lax.broadcasted_iota(jnp.int32, (128, TOK), 0)
    position = lax.div(index, 16) * 32 + lax.rem(index, 16)
    for g in range(2):
        u = jnp.sum(uacc[g], axis=1, keepdims=True)
        v = jnp.sum(vacc[g], axis=1, keepdims=True)
        q = (pacc[g] - u * mean_row) * rstd + v
        q = (q * lax.rsqrt(jnp.mean(q * q, axis=0, keepdims=True) + epsilon)).astype(BF16)
        exps = []
        for s2 in range(2):
            scores = jnp.dot(kvb[g, s2, 0], q, preferred_element_type=F32) / jnp.sqrt(F32(HD))
            live = position + 16 * s2 < length_ref[0]
            exps.append(jnp.where(live, jnp.exp(scores), 0.0))
        total = jnp.sum(exps[0], axis=0, keepdims=True) + jnp.sum(exps[1], axis=0, keepdims=True)
        inverse = 1.0 / total
        mixed = jnp.dot(
            kvb[g, 0, 1], (exps[0] * inverse).astype(BF16), preferred_element_type=F32
        ) + jnp.dot(kvb[g, 1, 1], (exps[1] * inverse).astype(BF16), preferred_element_type=F32)
        att[hid(g, y, c)] = mixed.astype(BF16)
        launch(att, r2s, r2r, b2s, b2r, g)
        wo_forward(1 + g)

    oacc[...] = jnp.zeros_like(oacc)

    def out_project(x2, y2):
        a = att[pl.ds(hid(x2, y2, 0), 2)].reshape(256, TOK)
        for g in range(2):
            oacc[g] += jnp.dot(wo[g, x2, y2], a, preferred_element_type=F32)

    def out_block(k):
        for off in offsets(k):
            i = yy(off)
            bridge_wait(att, b2s, b2r, i)
            out_wait(wo, ots, otr, i)
            out_project(p, i)
            fwd_wait(wo, ofs, ofr, i)
            out_project(np_, i)

    def att_step(g, k):
        ring_step(att, r2s, r2r, b2s, b2r, g, g == 0, k)

    att_step(0, 1)
    wo_forward(3)
    att_step(1, 1)
    out_block(0)
    att_step(0, 2)
    wo_forward(4)
    att_step(1, 2)
    out_block(1)
    wo_forward(5)
    att_step(0, 3)
    wo_forward(6)
    att_step(1, 3)
    out_block(2)
    att_step(0, 4)
    wo_forward(7)
    att_step(1, 4)
    out_block(3)
    out_block(4)

    half = pl.ds(pl.multiple_of(c * CH, CH), CH)

    def denoise(x2):
        gate = gcol[x2, half, :]
        gated = oacc[x2] * jnp.concatenate([gate, gate], axis=1)
        return (nz[hid(x2, y, c)].astype(F32) + gated).astype(BF16)

    def error_of(done, clean, noise):
        target = clean.astype(F32) - (1.0 - sigma_min) * noise.astype(F32)
        e = done.astype(F32) - target
        e = e * e
        e = jnp.sum(e.reshape(CH // 8, 8, TOK), axis=0)
        return e[:, 0:128] + e[:, 128:256]

    done = denoise(nx)
    xs2[...] = done
    error = error_of(done, nlat[...], nnoi[...])
    done = denoise(x)
    out_ref[:, mine] = done
    error = error + error_of(done, lat_ref[:, mine], noi_ref[:, mine])

    def slot(ss, xx, cc):
        return ss * 4 + xx * 2 + cc

    here = slot(s, x, c)
    l1[here] = error
    group = []
    for ds in range(2):
        for dx in range(2):
            for dc in range(2):
                if ds + dx + dc:
                    s2 = s if ds == 0 else 1 - s
                    x2 = x if dx == 0 else nx
                    c2 = c if dc == 0 else 1 - c
                    group.append((s2, x2, c2))
    for k, (s2, x2, c2) in enumerate(group):
        rcopy(
            l1.at[here], l1.at[here], l1s.at[k], l1r.at[here], {"head": hid(x2, y, c2), "seq": s2}
        ).start()
    xf = rcopy(xs2, xr2, xfs, xfr, inner)
    xf.start()
    for s2, x2, c2 in group:
        at = l1.at[slot(s2, x2, c2)]
        rcopy(at, at, l1s.at[0], l1r.at[slot(s2, x2, c2)], sib).wait_recv()
    l2[y] = jnp.sum(l1[...], axis=0)
    for off in range(1, YN):
        rcopy(
            l2.at[y], l2.at[y], l2s.at[off], l2r.at[y], {"head": hid(x, yy(off), c)}
        ).start()

    for j in range(4):
        for x2 in range(2):
            @pl.when(t1_remote(j, x2))
            def _(j=j, x2=x2):
                t1(j, x2).wait_send()
    xf.wait_recv()
    out_ref[:, theirs] = xr2[...]
    for copy in xe:
        copy.wait_send()
    for off in range(1, YN):
        t2(off).wait_send()
    kz.wait_send()
    for copy in kx:
        copy.wait_send()
    xf.wait_send()

    for i in range(YN):
        t_sib(i).wait_send()
        w_z(wq, wzs, wzr, i).wait_send()
        w_out(wq, wts, wtr, i).wait_send()
        w_fwd(wq, wfs, wfr, i).wait_send()
        w_z(wo, ozs, ozr, i).wait_send()
        w_out(wo, ots, otr, i).wait_send()
        w_fwd(wo, ofs, ofr, i).wait_send()
        for x2 in range(2):
            bridge(nz, b1s, b1r, x2, i).wait_send()
            bridge(att, b2s, b2r, x2, i).wait_send()
    for buf, rs, rr in ((nz, r1s, r1r), (att, r2s, r2r)):
        for x2 in range(2):
            rises = x2 == 0
            at = x2 if buf is att else (x if rises else nx)
            for k in range(4):
                if k < 3 or rises:
                    ring(buf, rs, rr, at, yy(8 - k), 0).wait_send()
                if k < 3 or not rises:
                    ring(buf, rs, rr, at, yy(k), 1).wait_send()
    for k, (s2, x2, c2) in enumerate(group):
        rcopy(l1.at[here], l1.at[here], l1s.at[k], l1r.at[here], sib).wait_send()

    for off in range(1, YN):
        at = l2.at[yy(off)]
        rcopy(at, at, l2s.at[off], l2r.at[yy(off)], sib).wait_recv()
    for off in range(1, YN):
        rcopy(l2.at[y], l2.at[y], l2s.at[off], l2r.at[y], sib).wait_send()
    loss_ref[0] = jnp.sum(jnp.sum(l2[...], axis=0)) / (1024 * D)


def local(
    text_hidden, text_length, latent, noise, level_index, mod_table, wq_halves, wo_halves, wkv_halves
):
    dma = pltpu.SemaphoreType.DMA
    vmem = pltpu.VMEM
    any_ = pl.BlockSpec(memory_space=pl.ANY)
    in_vmem = pl.BlockSpec(memory_space=pltpu.VMEM)
    in_smem = pl.BlockSpec(memory_space=pltpu.SMEM)
    in_hbm = pl.BlockSpec(memory_space=pltpu.HBM)
    out, loss = pl.pallas_call(
        kernel,
        out_shape=(
            jax.ShapeDtypeStruct((CH, 2 * TOK), BF16),
            jax.ShapeDtypeStruct((1,), F32),
        ),
        in_specs=[in_hbm] * 2 + [any_] * 7,
        out_specs=(in_vmem, in_smem),
        scratch_shapes=[
            pltpu.SMEM((1,), jnp.int32),
            pltpu.SMEM((1,), jnp.int32),
            vmem((32, 128), BF16),
            vmem((CH, 2 * TOK), BF16),
            vmem((CH, 2 * TOK), BF16),
            vmem((3, LEVELS, D), BF16),
            vmem((D // 2, HD), BF16),
            vmem((TD, HD), BF16),
            vmem((512, HD), F32),
            vmem((TD // 2, 256), BF16),
            vmem((2, 2, YN, CH, 256), BF16),
            vmem((2, 2, YN, HD, 384), BF16),
            vmem((32, CH, TOK), BF16),
            vmem((CH, TOK), BF16),
            vmem((CH, TOK), BF16),
            vmem((3, 16, 1, 384), F32),
            vmem((2, 384, 128), F32),
            vmem((YN, 128, 256), BF16),
            vmem((136, 256), F32),
            vmem((136, 256), F32),
            vmem((2, 2, 2, 128, 128), BF16),
            vmem((2, HD, TOK), F32),
            vmem((2, HD, 128), F32),
            vmem((2, HD, 128), F32),
            vmem((8, TOK), F32),
            vmem((8, TOK), F32),
            vmem((32, HD, TOK), BF16),
            vmem((2, CH, TOK), F32),
            vmem((CH, TOK), BF16),
            vmem((CH, TOK), BF16),
            vmem((8, 8, 128), F32),
            vmem((YN, 8, 128), F32),
            dma((8,)),
            dma((YN,)),
            dma((4, 2)),
            dma((ZN,)),
            dma((YN,)),
            dma((YN,)),
            dma((YN,)),
            dma((YN,)),
            dma((2,)),
            dma((2,)),
            dma((2, YN, 2)),
            dma((2, YN)),
            dma((2, YN)),
            dma((2, YN)),
            dma((YN,)),
            dma((YN,)),
            dma((YN,)),
            dma((YN,)),
            dma((YN,)),
            dma((YN,)),
            dma,
            dma,
            dma((3,)),
            dma((2, 2)),
            dma((2, YN, 2)),
            dma((2, YN)),
            dma((2, YN)),
            dma((2, YN)),
            dma((YN,)),
            dma((YN,)),
            dma((YN,)),
            dma((YN,)),
            dma((YN,)),
            dma((YN,)),
            dma,
            dma,
            dma((7,)),
            dma((8,)),
            dma((YN,)),
            dma((YN,)),
        ],
        compiler_params=pltpu.CompilerParams(
            collective_id=0, has_side_effects=True, vmem_limit_bytes=60 << 20
        ),
    )(
        level_index,
        text_length,
        text_hidden,
        jnp.swapaxes(latent[0], 0, 1),
        jnp.swapaxes(noise[0], 0, 1),
        jnp.swapaxes(mod_table, 1, 2),
        wq_halves[0],
        jnp.swapaxes(wo_halves[0], 0, 1),
        wkv_halves[0].reshape(TD, HD),
    )
    return (jnp.swapaxes(out, 0, 1)[None], loss)


def solution(mesh):
    return jax.shard_map(
        local,
        mesh=mesh,
        in_specs=(
            P("branch", "head"),
            P(),
            P("branch", "seq", "head"),
            P("branch", "seq", "head"),
            P("branch"),
            P(),
            P("branch", None, "head"),
            P("branch", None, "head"),
            P("branch", None, None, "head"),
        ),
        out_specs=(P("branch", "seq", "head"), P("branch")),
        check_vma=False,
    )
```

```python
import jax
import jax.numpy as jnp
from jax import lax
from jax.experimental import pallas as pl
from jax.experimental.pallas import tpu as pltpu
from jax.sharding import PartitionSpec as P

MESH = pl.DeviceIdType.MESH
F32 = jnp.float32
BF16 = jnp.bfloat16

D = 6144
TD = 4096
HD = 128
LEVELS = 8
YN = 8
ZN = 8
CH = 192
TOK = 256
epsilon = 1e-06
sigma_min = 1e-05

ORDER = (0, 1, 7, 2, 6, 3, 5, 4)


def hid(x, y, c):
    return x * 16 + y * 2 + c


def kernel(
    level_hbm,
    length_hbm,
    text_hbm,
    lat_hbm,
    noi_hbm,
    mod_hbm,
    wq_hbm,
    wo_hbm,
    wkv_hbm,
    out_ref,
    loss_ref,
    level_ref,
    length_ref,
    text_ref,
    lat_ref,
    noi_ref,
    modv,
    wqv,
    wkv2,
    wkvf,
    wkv,
    wo,
    wq,
    nz,
    nlat,
    nnoi,
    rows,
    gcol,
    tx,
    kvs,
    kvr,
    kvb,
    pacc,
    uacc,
    vacc,
    s1acc,
    s2acc,
    att,
    oacc,
    xs2,
    xr2,
    l1,
    l2,
    lsem,
    wosem,
    t1s,
    t1r,
    t2s,
    t2r,
    tss,
    tsr,
    xes,
    xer,
    r1s,
    r1r,
    b1s,
    b1r,
    wzs,
    wzr,
    wts,
    wtr,
    wfs,
    wfr,
    kzs,
    kzr,
    kxs,
    kxr,
    r2s,
    r2r,
    b2s,
    b2r,
    ozs,
    ozr,
    ots,
    otr,
    ofs,
    ofr,
    xfs,
    xfr,
    l1s,
    l1r,
    l2s,
    l2r,
):
    h = lax.axis_index("head")
    z = lax.axis_index("branch")
    s = lax.axis_index("seq")
    c = lax.rem(h, 2)
    y = lax.rem(lax.div(h, 2), YN)
    x = lax.div(h, 16)
    p = lax.rem(z, 2)
    nx = 1 - x
    np_ = 1 - p

    def yy(off):
        return lax.rem(y + off, YN)

    def rcopy(src, dst, ssem, rsem, dev):
        return pltpu.make_async_remote_copy(
            src_ref=src, dst_ref=dst, send_sem=ssem, recv_sem=rsem,
            device_id=dev, device_id_type=MESH,
        )

    sib = {"head": hid(x, y, 1 - c)}
    up = {"head": hid(x, yy(1), c)}
    down = {"head": hid(x, yy(7), c)}
    inner = {"head": hid(nx, y, c)}
    outer = {"head": hid(nx, y, c), "seq": 1 - s}
    far = {"seq": 1 - s}
    zpart = {"branch": z + 1 - 2 * p}

    barrier = pltpu.get_barrier_semaphore()
    peers = []
    for dz in (4, 3, 5, 2, 6, 1, 7, 0):
        for x2 in range(2):
            zt = lax.rem(z + dz, ZN)
            if dz == 0:
                if x2 == 0:
                    peers.append(inner)
            else:
                peers.append({"branch": zt, "head": hid(x2, y, c)})
    for off in (4, 3, 5, 2, 6, 1, 7):
        peers.append({"head": hid(x, yy(off), c)})
    peers.append(sib)
    peers.append({"head": hid(nx, y, 1 - c)})
    for xx in (x, nx):
        for cc in (c, 1 - c):
            peers.append({"head": hid(xx, y, cc), "seq": 1 - s})
    for dev in peers:
        pl.semaphore_signal(barrier, inc=1, device_id=dev, device_id_type=MESH)

    cp_mod = pltpu.make_async_copy(mod_hbm.at[lax.div(z, 2)], modv, lsem.at[0])
    cp_wq = pltpu.make_async_copy(wq_hbm, wqv, lsem.at[1])
    cp_wkv = pltpu.make_async_copy(wkv_hbm, wkv2, lsem.at[2])
    cp_lat = pltpu.make_async_copy(lat_hbm, lat_ref, lsem.at[3])
    cp_noi = pltpu.make_async_copy(noi_hbm, noi_ref, lsem.at[4])
    cp_text = pltpu.make_async_copy(text_hbm, text_ref, lsem.at[5])
    cp_level = pltpu.make_async_copy(level_hbm, level_ref, lsem.at[6])
    cp_length = pltpu.make_async_copy(length_hbm, length_ref, lsem.at[7])
    cp_level.start()
    cp_lat.start()
    cp_noi.start()
    cp_text.start()
    cp_length.start()
    cp_wq.start()
    cp_mod.start()
    cp_wkv.start()

    def cp_wo(i):
        return pltpu.make_async_copy(
            wo_hbm.at[:, pl.ds(i * 256, 256)], wo.at[x, p, i], wosem.at[i]
        )

    for i in range(YN):
        cp_wo(i).start()

    cp_level.wait()
    cp_length.wait()
    level_time = (level_ref[0].astype(F32) + 0.5) / LEVELS
    noise_level = 1.0 - (1.0 - sigma_min) * level_time
    mine = pl.ds(pl.multiple_of(x * TOK, TOK), TOK)
    theirs = pl.ds(pl.multiple_of(nx * TOK, TOK), TOK)

    def noisy_of(clean, noise):
        return (level_time * clean.astype(F32) + noise_level * noise.astype(F32)).astype(BF16)

    cp_lat.wait()
    cp_noi.wait()
    nz[h] = noisy_of(lat_ref[:, mine], noi_ref[:, mine])
    text_rows = pl.ds(pl.multiple_of(s * 16, 16), 16)
    my_rows = pl.ds(pl.multiple_of(z * 16, 16), 16)
    my_lanes = pl.ds(pl.multiple_of(c * 128, 128), 128)

    cp_text.wait()

    @pl.when(x == p)
    def _():
        tx[y, my_rows, my_lanes] = text_ref[text_rows, :]

    cp_wq.wait()

    def turn(i, carry):
        block = wqv[pl.ds(pl.multiple_of(i * 384, 384), 384), :]
        wq[x, p, i] = jnp.transpose(block.astype(F32)).astype(BF16)
        return carry

    lax.fori_loop(0, YN, turn, 0)

    pl.semaphore_wait(barrier, len(peers))

    def t1(j, x2):
        return rcopy(
            text_ref.at[text_rows, :], tx.at[y, my_rows, my_lanes],
            t1s.at[j, x2], t1r.at[z],
            {"branch": 2 * j + x, "head": hid(x2, y, c)},
        )

    def t1_remote(j, x2):
        return jnp.logical_or(2 * j + x != z, x2 != x)

    for j in range(4):
        for x2 in range(2):
            @pl.when(t1_remote(j, x2))
            def _(j=j, x2=x2):
                t1(j, x2).start()

    xe = [
        rcopy(lat_ref.at[:, theirs], nlat, xes.at[0], xer.at[0], inner),
        rcopy(noi_ref.at[:, theirs], nnoi, xes.at[1], xer.at[1], inner),
    ]

    def piece(buf, x2, y2):
        return buf.at[hid(x2, y2, c)]

    def ring(buf, ssem, rsem, x2, y2, way):
        at = piece(buf, x2, y2)
        return rcopy(at, at, ssem.at[x2, y2, way], rsem.at[x2, y2], up if way == 0 else down)

    def bridge(buf, ssem, rsem, x2, y2):
        at = piece(buf, x2, y2)
        return rcopy(at, at, ssem.at[x2, y2], rsem.at[x2, y2], sib)

    def launch(buf, rs, rr, bs, br, x2):
        ring(buf, rs, rr, x2, y, 0).start()
        ring(buf, rs, rr, x2, y, 1).start()
        bridge(buf, bs, br, x2, y).start()

    launch(nz, r1s, r1r, b1s, b1r, x)
    for copy in xe:
        copy.start()

    def w_z(buf, ssem, rsem, i):
        at = buf.at[x, p, i]
        return rcopy(at, at, ssem.at[i], rsem.at[i], zpart)

    def w_out(buf, ssem, rsem, i):
        at = buf.at[x, p, i]
        return rcopy(at, at, ssem.at[i], rsem.at[i], outer)

    def w_fwd(buf, ssem, rsem, i):
        at = buf.at[x, np_, i]
        return rcopy(at, at, ssem.at[i], rsem.at[i], inner)

    for off in ORDER:
        w_z(wq, wzs, wzr, yy(off)).start()
        w_out(wq, wts, wtr, yy(off)).start()

    cp_mod.wait()
    pick = (lax.broadcasted_iota(jnp.int32, (LEVELS, 1), 0) == level_ref[0]).astype(F32)
    for k in range(3):
        for i in range(16):
            row = jnp.sum(
                modv[k, :, i * 384 : (i + 1) * 384].astype(F32) * pick, axis=0, keepdims=True
            )
            rows[k, i] = row + 1.0 if k == 1 else row
    for x2 in range(2):
        gate = jnp.broadcast_to(rows[2, x2 * 8 + y], (128, 384))
        gcol[x2] = jnp.transpose(gate)

    def t1_wait(zs):
        rcopy(
            text_ref.at[text_rows, :],
            tx.at[y, pl.ds(zs * 16, 16), my_lanes],
            t1s.at[0, 0], t1r.at[zs], inner,
        ).wait_recv()

    def t2(off):
        at = tx.at[y, :, my_lanes]
        return rcopy(at, at, t2s.at[off], t2r.at[y], {"head": hid(x, yy(off), c)})

    def t2_wait(y2):
        at = tx.at[y2, :, my_lanes]
        rcopy(at, at, t2s.at[0], t2r.at[y2], sib).wait_recv()

    def t_sib(y2):
        at = tx.at[y2, :, my_lanes]
        return rcopy(at, at, tss.at[y2], tsr.at[y2], sib)

    def t_sib_wait(y2):
        at = tx.at[y2, :, pl.ds(pl.multiple_of((1 - c) * 128, 128), 128)]
        rcopy(at, at, tss.at[y2], tsr.at[y2], sib).wait_recv()

    pacc[...] = jnp.zeros_like(pacc)
    uacc[...] = jnp.zeros_like(uacc)
    vacc[...] = jnp.zeros_like(vacc)
    s1acc[...] = jnp.zeros_like(s1acc)
    s2acc[...] = jnp.zeros_like(s2acc)

    def project(x2, y2):
        chip = x2 * 8 + y2
        n = nz[pl.ds(hid(x2, y2, 0), 2)].reshape(384, TOK)
        scale = rows[1, chip]
        shift = rows[0, chip]
        for g in range(2):
            w = wq[g, x2, y2].astype(F32)
            ws = w * scale
            high = ws.astype(BF16)
            low = (ws - high.astype(F32)).astype(BF16)
            pacc[g] += jnp.dot(high, n, preferred_element_type=F32) + jnp.dot(
                low, n, preferred_element_type=F32
            )
            uacc[g] += ws[:, 0:128] + ws[:, 128:256] + ws[:, 256:384]
            sh = w * shift
            vacc[g] += sh[:, 0:128] + sh[:, 128:256] + sh[:, 256:384]
        nf = n.astype(F32).reshape(48, 8, TOK)
        s1acc[...] += jnp.sum(nf, axis=0)
        s2acc[...] += jnp.sum(nf * nf, axis=0)

    def ring_step(buf, rs, rr, bs, br, x2, rises, k):
        for way in range(2):
            last = rises if way == 0 else not rises
            y2 = yy(8 - k) if way == 0 else yy(k)
            if k < 4 or last:
                ring(buf, rs, rr, x2, y2, way).wait_recv()
                if k < 3 or (k == 3 and last):
                    ring(buf, rs, rr, x2, y2, way).start()
                bridge(buf, bs, br, x2, y2).start()

    def bridge_wait(buf, bs, br, y2):
        for x2 in range(2):
            at = buf.at[hid(x2, y2, 1 - c)]
            rcopy(at, at, bs.at[x2, y2], br.at[x2, y2], sib).wait_recv()

    def fwd_wait(buf, fs, fr, i):
        at = buf.at[nx, np_, i]
        rcopy(at, at, fs.at[i], fr.at[i], inner).wait_recv()

    def out_wait(buf, os_, or_, i):
        at = buf.at[nx, p, i]
        rcopy(at, at, os_.at[i], or_.at[i], outer).wait_recv()

    def z_forward(buf, zs, zr, fs, fr, i):
        at = buf.at[x, np_, i]
        rcopy(at, at, zs.at[i], zr.at[i], zpart).wait_recv()
        w_fwd(buf, fs, fr, i).start()

    def offsets(k):
        return (k,) if k in (0, 4) else (k, 8 - k)

    def query_block(k):
        for off in offsets(k):
            i = yy(off)
            bridge_wait(nz, b1s, b1r, i)
            out_wait(wq, wts, wtr, i)
            project(p, i)
            fwd_wait(wq, wfs, wfr, i)
            project(np_, i)

    def wq_forward(j):
        z_forward(wq, wzs, wzr, wfs, wfr, yy(ORDER[j]))

    def wo_forward(j):
        z_forward(wo, ozs, ozr, ofs, ofr, yy(ORDER[j]))

    def own_step(k):
        ring_step(nz, r1s, r1r, b1s, b1r, x, True, k)

    def next_step(k):
        ring_step(nz, r1s, r1r, b1s, b1r, nx, False, k)

    own_step(1)
    wq_forward(0)
    for zs in range(ZN):
        @pl.when(jnp.logical_or(x != p, z != zs))
        def _(zs=zs):
            t1_wait(zs)
    for off in (4, 3, 5, 2, 6, 1, 7):
        t2(off).start()
    t_sib(y).start()
    for copy in xe:
        copy.wait_recv()
    nz[hid(nx, y, c)] = noisy_of(nlat[...], nnoi[...])
    launch(nz, r1s, r1r, b1s, b1r, nx)
    wq_forward(1)
    own_step(2)
    wq_forward(2)

    cp_wkv.wait()

    def spread(i, carry):
        at = pl.ds(pl.multiple_of(i * 512, 512), 512)
        wkvf[...] = wkv2[at, :].astype(F32)
        to = pl.ds(pl.multiple_of(i * 256, 256), 256)
        wkv[to, 0:128] = wkvf[pl.ds(0, 256, stride=2), :].astype(BF16)
        wkv[to, 128:256] = wkvf[pl.ds(1, 256, stride=2), :].astype(BF16)
        return carry

    lax.fori_loop(0, YN, spread, 0)

    next_step(1)
    wq_forward(3)
    for off in (1, 7, 2, 6, 3, 5, 4):
        t2_wait(yy(off))
        t_sib(yy(off)).start()
    wq_forward(4)

    kvs[0:128, :] = jnp.zeros((128, 256), F32)
    squares = jnp.zeros((128, 256), F32)
    for off in ORDER:
        y2 = yy(off)
        t_sib_wait(y2)
        t = tx[y2]
        kvs[0:128, :] += jnp.dot(
            t, wkv[pl.ds(pl.multiple_of(y2 * 256, 256), 256), :], preferred_element_type=F32
        )
        tf = t.astype(F32)
        squares = squares + tf * tf
    square_col = jnp.sum(squares, axis=1, keepdims=True)
    square_row = jnp.transpose(jnp.broadcast_to(square_col, (128, 128)))[0:8]
    kvs[128:136, 0:128] = square_row
    kvs[128:136, 128:256] = square_row
    kz = rcopy(kvs, kvr, kzs, kzr, zpart)
    kz.start()

    for i in range(YN):
        cp_wo(i).wait()
    for off in ORDER:
        w_z(wo, ozs, ozr, yy(off)).start()
    w_out(wo, ots, otr, yy(ORDER[0])).start()

    own_step(3)
    wq_forward(5)
    next_step(2)
    wq_forward(6)
    query_block(0)
    query_block(1)

    kz.wait_recv()
    other_col = jnp.transpose(jnp.broadcast_to(kvr[128:129, 0:128], (128, 128)))[:, 0:1]
    text_rstd = lax.rsqrt((square_col + other_col) / TD + epsilon)
    text_proj = (kvs[0:128, :] + kvr[0:128, :]) * text_rstd
    keys = text_proj[:, 0:128]
    keys = keys * lax.rsqrt(jnp.mean(keys * keys, axis=1, keepdims=True) + epsilon)
    kvb[x, s, 0] = keys.astype(BF16)
    kvb[x, s, 1] = jnp.transpose(text_proj[:, 128:256]).astype(BF16)
    kx = [
        rcopy(kvb.at[x, s], kvb.at[x, s], kxs.at[k], kxr.at[x, s], dev)
        for k, dev in enumerate((inner, far, outer))
    ]
    for copy in kx:
        copy.start()

    for off in ORDER[1:]:
        w_out(wo, ots, otr, yy(off)).start()
    own_step(4)
    next_step(3)
    wq_forward(7)
    query_block(2)
    query_block(3)
    next_step(4)
    wo_forward(0)
    query_block(4)

    for x2, s2 in ((nx, s), (x, 1 - s), (nx, 1 - s)):
        at = kvb.at[x2, s2]
        rcopy(at, at, kxs.at[0], kxr.at[x2, s2], inner).wait_recv()
    mean_row = jnp.sum(s1acc[...], axis=0, keepdims=True) / D
    var_row = jnp.sum(s2acc[...], axis=0, keepdims=True) / D - mean_row * mean_row
    rstd = lax.rsqrt(var_row + epsilon)
    index = lax.broadcasted_iota(jnp.int32, (128, TOK), 0)
    position = lax.div(index, 16) * 32 + lax.rem(index, 16)
    for g in range(2):
        u = jnp.sum(uacc[g], axis=1, keepdims=True)
        v = jnp.sum(vacc[g], axis=1, keepdims=True)
        q = (pacc[g] - u * mean_row) * rstd + v
        q = (q * lax.rsqrt(jnp.mean(q * q, axis=0, keepdims=True) + epsilon)).astype(BF16)
        exps = []
        for s2 in range(2):
            scores = jnp.dot(kvb[g, s2, 0], q, preferred_element_type=F32) / jnp.sqrt(F32(HD))
            live = position + 16 * s2 < length_ref[0]
            exps.append(jnp.where(live, jnp.exp(scores), 0.0))
        total = jnp.sum(exps[0], axis=0, keepdims=True) + jnp.sum(exps[1], axis=0, keepdims=True)
        inverse = 1.0 / total
        mixed = jnp.dot(
            kvb[g, 0, 1], (exps[0] * inverse).astype(BF16), preferred_element_type=F32
        ) + jnp.dot(kvb[g, 1, 1], (exps[1] * inverse).astype(BF16), preferred_element_type=F32)
        att[hid(g, y, c)] = mixed.astype(BF16)
        launch(att, r2s, r2r, b2s, b2r, g)
        wo_forward(1 + g)

    oacc[...] = jnp.zeros_like(oacc)

    def out_project(x2, y2):
        a = att[pl.ds(hid(x2, y2, 0), 2)].reshape(256, TOK)
        for g in range(2):
            oacc[g] += jnp.dot(wo[g, x2, y2], a, preferred_element_type=F32)

    def out_block(k):
        for off in offsets(k):
            i = yy(off)
            bridge_wait(att, b2s, b2r, i)
            out_wait(wo, ots, otr, i)
            out_project(p, i)
            fwd_wait(wo, ofs, ofr, i)
            out_project(np_, i)

    def att_step(g, k):
        ring_step(att, r2s, r2r, b2s, b2r, g, g == 0, k)

    att_step(0, 1)
    wo_forward(3)
    att_step(1, 1)
    out_block(0)
    att_step(0, 2)
    wo_forward(4)
    att_step(1, 2)
    out_block(1)
    wo_forward(5)
    att_step(0, 3)
    wo_forward(6)
    att_step(1, 3)
    out_block(2)
    att_step(0, 4)
    wo_forward(7)
    att_step(1, 4)
    out_block(3)
    out_block(4)

    half = pl.ds(pl.multiple_of(c * CH, CH), CH)

    def denoise(x2):
        gate = gcol[x2, half, :]
        gated = oacc[x2] * jnp.concatenate([gate, gate], axis=1)
        return (nz[hid(x2, y, c)].astype(F32) + gated).astype(BF16)

    def error_of(done, clean, noise):
        target = clean.astype(F32) - (1.0 - sigma_min) * noise.astype(F32)
        e = done.astype(F32) - target
        e = e * e
        e = jnp.sum(e.reshape(CH // 8, 8, TOK), axis=0)
        return e[:, 0:128] + e[:, 128:256]

    done = denoise(nx)
    xs2[...] = done
    error = error_of(done, nlat[...], nnoi[...])
    done = denoise(x)
    out_ref[:, mine] = done
    error = error + error_of(done, lat_ref[:, mine], noi_ref[:, mine])

    def slot(ss, xx, cc):
        return ss * 4 + xx * 2 + cc

    here = slot(s, x, c)
    l1[here] = error
    group = []
    for ds in range(2):
        for dx in range(2):
            for dc in range(2):
                if ds + dx + dc:
                    s2 = s if ds == 0 else 1 - s
                    x2 = x if dx == 0 else nx
                    c2 = c if dc == 0 else 1 - c
                    group.append((s2, x2, c2))
    for k, (s2, x2, c2) in enumerate(group):
        rcopy(
            l1.at[here], l1.at[here], l1s.at[k], l1r.at[here], {"head": hid(x2, y, c2), "seq": s2}
        ).start()
    xf = rcopy(xs2, xr2, xfs, xfr, inner)
    xf.start()
    for s2, x2, c2 in group:
        at = l1.at[slot(s2, x2, c2)]
        rcopy(at, at, l1s.at[0], l1r.at[slot(s2, x2, c2)], sib).wait_recv()
    l2[y] = jnp.sum(l1[...], axis=0)
    for off in range(1, YN):
        rcopy(
            l2.at[y], l2.at[y], l2s.at[off], l2r.at[y], {"head": hid(x, yy(off), c)}
        ).start()

    for j in range(4):
        for x2 in range(2):
            @pl.when(t1_remote(j, x2))
            def _(j=j, x2=x2):
                t1(j, x2).wait_send()
    xf.wait_recv()
    out_ref[:, theirs] = xr2[...]
    for copy in xe:
        copy.wait_send()
    for off in range(1, YN):
        t2(off).wait_send()
    kz.wait_send()
    for copy in kx:
        copy.wait_send()
    xf.wait_send()

    for i in range(YN):
        t_sib(i).wait_send()
        w_z(wq, wzs, wzr, i).wait_send()
        w_out(wq, wts, wtr, i).wait_send()
        w_fwd(wq, wfs, wfr, i).wait_send()
        w_z(wo, ozs, ozr, i).wait_send()
        w_out(wo, ots, otr, i).wait_send()
        w_fwd(wo, ofs, ofr, i).wait_send()
        for x2 in range(2):
            bridge(nz, b1s, b1r, x2, i).wait_send()
            bridge(att, b2s, b2r, x2, i).wait_send()
    for buf, rs, rr in ((nz, r1s, r1r), (att, r2s, r2r)):
        for x2 in range(2):
            rises = x2 == 0
            at = x2 if buf is att else (x if rises else nx)
            for k in range(4):
                if k < 3 or rises:
                    ring(buf, rs, rr, at, yy(8 - k), 0).wait_send()
                if k < 3 or not rises:
                    ring(buf, rs, rr, at, yy(k), 1).wait_send()
    for k, (s2, x2, c2) in enumerate(group):
        rcopy(l1.at[here], l1.at[here], l1s.at[k], l1r.at[here], sib).wait_send()

    for off in range(1, YN):
        at = l2.at[yy(off)]
        rcopy(at, at, l2s.at[off], l2r.at[yy(off)], sib).wait_recv()
    for off in range(1, YN):
        rcopy(l2.at[y], l2.at[y], l2s.at[off], l2r.at[y], sib).wait_send()
    loss_ref[0] = jnp.sum(jnp.sum(l2[...], axis=0)) / (1024 * D)


def local(
    text_hidden, text_length, latent, noise, level_index, mod_table, wq_halves, wo_halves, wkv_halves
):
    dma = pltpu.SemaphoreType.DMA
    vmem = pltpu.VMEM
    any_ = pl.BlockSpec(memory_space=pl.ANY)
    in_vmem = pl.BlockSpec(memory_space=pltpu.VMEM)
    in_smem = pl.BlockSpec(memory_space=pltpu.SMEM)
    in_hbm = pl.BlockSpec(memory_space=pltpu.HBM)
    out, loss = pl.pallas_call(
        kernel,
        out_shape=(
            jax.ShapeDtypeStruct((CH, 2 * TOK), BF16),
            jax.ShapeDtypeStruct((1,), F32),
        ),
        in_specs=[in_hbm] * 2 + [any_] * 7,
        out_specs=(in_vmem, in_smem),
        scratch_shapes=[
            pltpu.SMEM((1,), jnp.int32),
            pltpu.SMEM((1,), jnp.int32),
            vmem((32, 128), BF16),
            vmem((CH, 2 * TOK), BF16),
            vmem((CH, 2 * TOK), BF16),
            vmem((3, LEVELS, D), BF16),
            vmem((D // 2, HD), BF16),
            vmem((TD, HD), BF16),
            vmem((512, HD), F32),
            vmem((TD // 2, 256), BF16),
            vmem((2, 2, YN, CH, 256), BF16),
            vmem((2, 2, YN, HD, 384), BF16),
            vmem((32, CH, TOK), BF16),
            vmem((CH, TOK), BF16),
            vmem((CH, TOK), BF16),
            vmem((3, 16, 1, 384), F32),
            vmem((2, 384, 128), F32),
            vmem((YN, 128, 256), BF16),
            vmem((136, 256), F32),
            vmem((136, 256), F32),
            vmem((2, 2, 2, 128, 128), BF16),
            vmem((2, HD, TOK), F32),
            vmem((2, HD, 128), F32),
            vmem((2, HD, 128), F32),
            vmem((8, TOK), F32),
            vmem((8, TOK), F32),
            vmem((32, HD, TOK), BF16),
            vmem((2, CH, TOK), F32),
            vmem((CH, TOK), BF16),
            vmem((CH, TOK), BF16),
            vmem((8, 8, 128), F32),
            vmem((YN, 8, 128), F32),
            dma((8,)),
            dma((YN,)),
            dma((4, 2)),
            dma((ZN,)),
            dma((YN,)),
            dma((YN,)),
            dma((YN,)),
            dma((YN,)),
            dma((2,)),
            dma((2,)),
            dma((2, YN, 2)),
            dma((2, YN)),
            dma((2, YN)),
            dma((2, YN)),
            dma((YN,)),
            dma((YN,)),
            dma((YN,)),
            dma((YN,)),
            dma((YN,)),
            dma((YN,)),
            dma,
            dma,
            dma((3,)),
            dma((2, 2)),
            dma((2, YN, 2)),
            dma((2, YN)),
            dma((2, YN)),
            dma((2, YN)),
            dma((YN,)),
            dma((YN,)),
            dma((YN,)),
            dma((YN,)),
            dma((YN,)),
            dma((YN,)),
            dma,
            dma,
            dma((7,)),
            dma((8,)),
            dma((YN,)),
            dma((YN,)),
        ],
        compiler_params=pltpu.CompilerParams(
            collective_id=0, has_side_effects=True, vmem_limit_bytes=60 << 20
        ),
    )(
        level_index,
        text_length,
        text_hidden,
        jnp.swapaxes(latent[0], 0, 1),
        jnp.swapaxes(noise[0], 0, 1),
        jnp.swapaxes(mod_table, 1, 2),
        wq_halves[0],
        jnp.swapaxes(wo_halves[0], 0, 1),
        wkv_halves[0].reshape(TD, HD),
    )
    return (jnp.swapaxes(out, 0, 1)[None], loss)


def solution(mesh):
    return jax.shard_map(
        local,
        mesh=mesh,
        in_specs=(
            P("branch", "head"),
            P(),
            P("branch", "seq", "head"),
            P("branch", "seq", "head"),
            P("branch"),
            P(),
            P("branch", None, "head"),
            P("branch", None, "head"),
            P("branch", None, None, "head"),
        ),
        out_specs=(P("branch", "seq", "head"), P("branch")),
        check_vma=False,
    )
```
